32 devices in a mesh: row: 4 (over y, core), col: 8 (over z, x).
Axes of the slice: x: 2, y: 2, z: 4, core: 2. Of those that a mesh axis runs over, the one named last changes fastest.
Arguments:
- gradient: bfloat16 [3584, 12288], P('row', 'col'), may hold values from -54 to 54
- momentum: float32 [3584, 12288], P('row', 'col'), may hold values from -54 to 54
Outputs:
- update_matrix: bfloat16 [3584, 12288], P('row', 'col')
- new_momentum: float32 [3584, 12288], P('row', 'col')
The draws below stay inside these ranges and needn't reach their ends.
All inputs are finite; a program needn't handle non-finite values.
Results may differ from the reference program's by a relative error of at most 0.013.
Values may be sent and summed in bfloat16 or wider, within the bound.
A program may use at most 128 MiB of HBM per device.

```python
import math
import jax
import jax.numpy as jnp

M = 3584
N = 12288
ITERS = 2


def ramped_rows(key):
    first, second = jax.random.split(key)
    position = jnp.arange(M).astype(jnp.float32) / M
    trend = jnp.exp(position * math.log(3.0))[:, None]
    factor = jnp.exp(jax.random.uniform(first, (M, 1), jnp.float32) * math.log(3.0))
    noise = jnp.clip(jax.random.normal(second, (M, N), jnp.float32), -4.0, 4.0)
    values = noise + 0.5 * jnp.roll(noise, M // 2, axis=0)
    return values * trend * factor


def draw_gradient(key, part):
    return ramped_rows(jax.random.fold_in(key, 11)).astype(jnp.bfloat16)


def draw_momentum(key, part):
    return ramped_rows(jax.random.fold_in(key, 23)).astype(jnp.float32)


def setup_inputs(seed: int = 0) -> dict:
    key_of = jax.random.split(jax.random.key(seed), 3)
    gradient = draw_gradient(jax.random.fold_in(key_of[2], 71), 0)
    momentum = draw_momentum(jax.random.fold_in(key_of[2], 71), 0)
    return {"gradient": gradient, "momentum": momentum}


MOMENTUM_DECAY = 0.95
EPSILON = 1e-07
COEF_LINEAR = 3.4445
COEF_CUBIC = -4.775
COEF_QUINTIC = 2.0315

def reference(gradient, momentum):
    grad32 = gradient.astype(jnp.float32)
    buffer = MOMENTUM_DECAY * momentum + grad32
    nesterov = grad32 + MOMENTUM_DECAY * buffer
    base = nesterov.astype(jnp.bfloat16)
    raw = jnp.dot(base, base.T, preferred_element_type=jnp.float32)
    quartic = jnp.sum(raw * raw)
    scale = 1.0 / jnp.sqrt(jnp.sqrt(quartic) + EPSILON)
    iterate = (base.astype(jnp.float32) * scale).astype(jnp.bfloat16)
    combined = iterate.astype(jnp.float32)
    for iteration in range(ITERS):
        if iteration == 0:
            gram = (raw * (scale * scale)).astype(jnp.bfloat16)
        else:
            gram = jnp.dot(iterate, iterate.T, preferred_element_type=jnp.float32).astype(jnp.bfloat16)
        product = jnp.dot(gram, iterate, preferred_element_type=jnp.float32)
        second = jnp.dot(gram, product.astype(jnp.bfloat16), preferred_element_type=jnp.float32)
        combined = COEF_LINEAR * iterate.astype(jnp.float32) + COEF_CUBIC * product + COEF_QUINTIC * second
        if iteration + 1 < ITERS:
            iterate = combined.astype(jnp.bfloat16)
    update_matrix = (combined * (0.2 * math.sqrt(max(M, N)))).astype(jnp.bfloat16)
    return (update_matrix, buffer)
```

```python
import functools
import math

import jax
import jax.numpy as jnp
from jax import lax
from jax.experimental import pallas as pl
from jax.experimental.pallas import tpu as pltpu
from jax.sharding import PartitionSpec as P

ITERS = 2

MOMENTUM_DECAY = 0.95
EPSILON = 1e-07
COEF_LINEAR = 3.4445
COEF_CUBIC = -4.775
COEF_QUINTIC = 2.0315


def outer_rows(left, right):
    return lax.dot_general(
        left, right, (((1,), (1,)), ((), ())), preferred_element_type=jnp.float32
    )


def direct_blocks(rows, block):
    if rows == 1:
        return [(0, 0, block, 0, 0)]
    half = block // 2
    middle = rows // 2
    found = []
    for j in range(rows):
        for offset in range(middle):
            i = (j + offset) % rows
            found.append((j, offset * block, block, i * block, j * block))
        low, high = min(j, (j + middle) % rows), max(j, (j + middle) % rows)
        top = low * block + (0 if j == low else half)
        found.append((j, middle * block, half, top, high * block))
    return found


def mirrored_blocks(rows):
    if rows == 1:
        return []
    middle = rows // 2
    pairs = [((j + k) % rows, j) for j in range(rows) for k in range(1, middle)]
    return pairs + [(low, low + middle) for low in range(middle)]


def chain_kernel(
    tile, factor, rows, shares_ref, x_ref, out_ref, gram_ref, first, one, two, rough, exact, total, sems
):
    size = gram_ref.shape[0]
    block = size // rows
    stride = shares_ref.shape[0] // rows
    strip = 128
    copies = []
    for number, (owner, start, height, row, column) in enumerate(direct_blocks(rows, block)):
        copies.append(
            pltpu.make_async_copy(
                shares_ref.at[pl.ds(owner * stride + start, height), :],
                gram_ref.at[pl.ds(row, height), pl.ds(column, block)],
                sems.at[number],
            )
        )
    for copy in copies:
        copy.start()
    for copy in copies:
        copy.wait()

    def squares(i, j, mirror):
        def body(step, carry):
            lanes = pl.ds(pl.multiple_of(j * block + step * strip, strip), strip)
            piece = gram_ref[pl.ds(i * block, block), lanes]
            if mirror:
                gram_ref[lanes, pl.ds(i * block, block)] = piece.T
            wide = piece.astype(jnp.float32)
            return carry + jnp.sum(wide * wide, axis=0, keepdims=True)

        return lax.fori_loop(0, block // strip, body, jnp.zeros((1, strip), jnp.float32))

    diagonal = sum(squares(i, i, False) for i in range(rows))
    others = sum(squares(i, j, True) for i, j in mirrored_blocks(rows)) + jnp.zeros_like(diagonal)
    quartic = jnp.sum(diagonal + 2.0 * others, axis=1, keepdims=True)
    scale = 1.0 / jnp.sqrt(jnp.sqrt(quartic) + EPSILON)
    square = scale * scale

    def times_gram(source, finish):
        @pl.loop(0, size // tile)
        def _(step):
            columns = pl.ds(pl.multiple_of(step * tile, tile), tile)
            value = jnp.dot(
                source[...], gram_ref[:, columns], preferred_element_type=jnp.float32
            )
            finish(columns, value * square)

    def polynomial(source, target):
        def keep(columns, value):
            exact[:, columns] = value
            rough[:, columns] = value.astype(jnp.bfloat16)

        def combine(columns, value):
            target[:, columns] = (
                COEF_LINEAR * source[:, columns].astype(jnp.float32)
                + COEF_CUBIC * exact[:, columns]
                + COEF_QUINTIC * value
            ).astype(jnp.bfloat16)

        times_gram(source, keep)
        times_gram(rough, combine)

    width = x_ref.shape[1]
    lanes_step = 128 if width % 128 == 0 else width

    @pl.loop(0, size // strip)
    def _(step):
        chunk = pl.ds(pl.multiple_of(step * strip, strip), strip)
        for lane in range(0, width, lanes_step):
            two[lane : lane + lanes_step, chunk] = x_ref[chunk, lane : lane + lanes_step].T

    polynomial(two, first)
    polynomial(first, one)
    polynomial(one, two)

    def after_product(columns, value):
        total[:, columns] = (
            COEF_LINEAR * first[:, columns].astype(jnp.float32) + COEF_CUBIC * value
        )
        one[:, columns] = value.astype(jnp.bfloat16)

    times_gram(two, after_product)
    polynomial(one, two)
    polynomial(two, one)

    def after_second(columns, value):
        two[:, columns] = (
            (total[:, columns] + COEF_QUINTIC * value) * (scale * factor)
        ).astype(jnp.bfloat16)

    times_gram(one, after_second)

    @pl.loop(0, size // strip)
    def _(step):
        chunk = pl.ds(pl.multiple_of(step * strip, strip), strip)
        for lane in range(0, width, lanes_step):
            out_ref[chunk, lane : lane + lanes_step] = two[lane : lane + lanes_step, chunk].T


def chain(shares, slab, factor, rows):
    size, width = slab.shape
    tile = 512 if size % 512 == 0 else size
    vmem = pl.BlockSpec(memory_space=pltpu.VMEM)
    half = pltpu.VMEM((width, size), jnp.bfloat16)
    full = pltpu.VMEM((width, size), jnp.float32)
    count = rows * (rows // 2 + 1)
    return pl.pallas_call(
        functools.partial(chain_kernel, tile, factor, rows),
        out_shape=jax.ShapeDtypeStruct((size, width), jnp.bfloat16),
        in_specs=[pl.BlockSpec(memory_space=pl.ANY), vmem],
        out_specs=vmem,
        scratch_shapes=[pltpu.VMEM((size, size), jnp.bfloat16)]
        + [half, half, half, half, full, full, pltpu.SemaphoreType.DMA((count,))],
        compiler_params=pltpu.CompilerParams(vmem_limit_bytes=63 * 1024 * 1024),
        name="chain",
    )(shares, slab)


def assembled(shares, rows, block):
    half = block // 2
    middle = rows // 2

    def at(i, j):
        offset = (i - j) % rows
        if offset < middle:
            return shares[j, offset * block : (offset + 1) * block]
        if offset > middle:
            return at(j, i).T
        low, high = min(i, j), max(i, j)
        value = jnp.concatenate([shares[low, -half:], shares[high, -half:]], axis=0)
        return value if i == low else value.T

    return jnp.concatenate(
        [
            jnp.concatenate([at(i, j) for j in range(rows)], axis=1)
            for i in range(rows)
        ],
        axis=0,
    )


def ring_kernel(partial_ref, out_ref, *scratch):
    landed, running, send_sems, recv_sems = scratch[:2], scratch[2:4], scratch[4], scratch[5]
    count = partial_ref.shape[0]
    column = lax.axis_index("col")
    odd, pair = lax.rem(column, 2), lax.div(column, 2)
    place = (1 - odd) * pair + odd * (count - 1 - pair)
    sign = 1 - 2 * lax.rem(lax.axis_index("row"), 2)
    ways = (sign, -sign)
    wide = landed[0].shape[2]
    lanes = (pl.ds(0, wide), pl.ds(wide, landed[1].shape[2]))

    def column_at(spot):
        spot = lax.rem(spot + 2 * count, count)
        back = lax.div(spot, count // 2)
        return (1 - back) * 2 * spot + back * (2 * (count - 1 - spot) + 1)

    barrier = pltpu.get_barrier_semaphore()
    for way in ways:
        pl.semaphore_signal(
            barrier,
            inc=1,
            device_id={"col": column_at(place + way)},
            device_id_type=pl.DeviceIdType.MESH,
        )
    pl.semaphore_wait(barrier, 2)

    def copy_of(step, k, source):
        return pltpu.make_async_remote_copy(
            src_ref=source,
            dst_ref=landed[k].at[step],
            send_sem=send_sems.at[k, step],
            recv_sem=recv_sems.at[k, step],
            device_id={"col": column_at(place + ways[k])},
            device_id_type=pl.DeviceIdType.MESH,
        )

    copies = []
    for k in range(2):
        source = partial_ref.at[column_at(place - ways[k]), :, lanes[k]]
        copies.append([copy_of(0, k, source)])
        copies[k][0].start()
    for step in range(count - 1):
        for k in range(2):
            copies[k][step].wait_recv()
            mine = partial_ref[column_at(place - ways[k] * (step + 2)), :, lanes[k]]
            value = landed[k][step].astype(jnp.float32) + mine.astype(jnp.float32)
            value = value.astype(jnp.bfloat16)
            if step < count - 2:
                running[k][step] = value
                copies[k].append(copy_of(step + 1, k, running[k].at[step]))
                copies[k][step + 1].start()
            else:
                out_ref[:, lanes[k]] = value
    for k in range(2):
        for copy in copies[k]:
            copy.wait_send()


def ring_sum(partial_value, count):
    block = partial_value.shape[1]
    height = partial_value.shape[0] // count
    wide = (block // 128 + 1) // 2 * 128
    vmem = pl.BlockSpec(memory_space=pltpu.VMEM)
    slots = [
        pltpu.VMEM((count - 1, height, width), jnp.bfloat16) for width in (wide, block - wide)
    ]
    sems = pltpu.SemaphoreType.DMA((2, count - 1))
    return pl.pallas_call(
        ring_kernel,
        out_shape=jax.ShapeDtypeStruct((height, block), jnp.bfloat16),
        in_specs=[vmem],
        out_specs=vmem,
        scratch_shapes=slots + slots + [sems, sems],
        compiler_params=pltpu.CompilerParams(
            collective_id=0, has_side_effects=True, vmem_limit_bytes=40 * 1024 * 1024
        ),
        name="ring_sum",
    )(partial_value.reshape(count, height, block))


LANES = 128


def ring_place(column, count):
    odd, pair = lax.rem(column, 2), lax.div(column, 2)
    return (1 - odd) * pair + odd * (count - 1 - pair)


def ring_column(spot, count):
    spot = lax.rem(spot + 2 * count, count)
    back = lax.div(spot, count // 2)
    return (1 - back) * 2 * spot + back * (2 * (count - 1 - spot) + 1)


def flipped(row, bits):
    chip, core = lax.div(row, 2), lax.rem(row, 2)
    if bits & 2:
        chip = 1 - chip
    if bits & 1:
        core = 1 - core
    return 2 * chip + core


def meet(barrier, targets):
    for target in targets:
        pl.semaphore_signal(
            barrier, inc=1, device_id=target, device_id_type=pl.DeviceIdType.MESH
        )
    pl.semaphore_wait(barrier, len(targets))


def remote(source, target, send_sem, recv_sem, device):
    return pltpu.make_async_remote_copy(
        src_ref=source,
        dst_ref=target,
        send_sem=send_sem,
        recv_sem=recv_sem,
        device_id=device,
        device_id_type=pl.DeviceIdType.MESH,
    )


def share_kernel(
    count, wide, base_ref, share_ref, slab_ref, panel, partial, landed, running,
    panel_send, panel_recv, own_sem, ring_send, ring_recv,
):
    chunks = panel.shape[1]
    block = chunks * LANES
    strip = block // count
    width = panel.shape[3] // 4
    me, column = lax.axis_index("row"), lax.axis_index("col")
    core = lax.rem(me, 2)
    place = ring_place(column, count)
    sign = 1 - 2 * core
    ways = (sign, -sign)
    meet(
        pltpu.get_barrier_semaphore(),
        [{"col": ring_column(place + way, count)} for way in ways]
        + [{"row": flipped(me, 1)}, {"row": flipped(me, 2)}],
    )

    def pass_on(slot, source, chunk):
        return remote(
            source,
            panel.at[slot, chunk],
            panel_send.at[slot - 1, chunk],
            panel_recv.at[slot - 1, chunk],
            {"row": flipped(me, 2 if slot == 2 else 1)},
        )

    own = pltpu.make_async_copy(base_ref, panel.at[0], own_sem)
    own.start()
    for chunk in range(chunks):
        pass_on(2, base_ref.at[chunk], chunk).start()
        pass_on(1, base_ref.at[chunk], chunk).start()
    own.wait()

    @pl.loop(0, 4 * chunks)
    def _(event):
        far = event >= 2 * chunks
        late = lax.max(event - 2 * chunks, 0)
        slot = jnp.where(far, 2 + lax.rem(late, 2), lax.div(event, chunks))
        chunk = jnp.where(far, lax.div(late, 2), lax.rem(event, chunks))
        for x in range(1, 4):
            @pl.when(slot == x)
            def _():
                pass_on(x, panel.at[2 if x == 3 else 0, chunk], chunk).wait_recv()
                if x == 2:
                    pass_on(3, panel.at[2, chunk], chunk).start()

        turned = lax.rem(slot, 2)
        offset = jnp.where(
            slot == 2, 2, turned * (2 - (1 - 2 * core) * (2 - slot))
        )
        owner = lax.rem(me + offset, 4)
        piece = panel[slot, chunk]
        target = pl.ds(pl.multiple_of((owner * chunks + chunk) * LANES, LANES), LANES)
        mine = pl.ds(pl.multiple_of(me * width, LANES), width)
        slab_ref[:, target] = panel[slot, chunk, :, mine].T
        spot = offset * chunks + chunk

        @pl.when(spot < chunks + wide - 1)
        def _():
            value = outer_rows(panel[0].reshape(block, panel.shape[3]), piece)
            value = value.astype(jnp.bfloat16)
            for c in range(count):
                place_in = spot - c * strip // LANES

                @pl.when((place_in >= 0) & (place_in < wide))
                def _():
                    lanes = pl.ds(pl.multiple_of(place_in * LANES, LANES), LANES)
                    partial[c, :, lanes] = value[c * strip : (c + 1) * strip]

    for slot in range(1, 4):
        for chunk in range(chunks):
            pass_on(slot, panel.at[2 if slot == 3 else 0, chunk], chunk).wait_send()

    streams = landed.shape[0]
    size = landed.shape[3]

    def ring_copy(step, k, source):
        return remote(
            source,
            landed.at[k, step],
            ring_send.at[k, step],
            ring_recv.at[k, step],
            {"col": ring_column(place + ways[k % 2], count)},
        )

    copies = []
    for k in range(streams):
        lanes = pl.ds(k * size, size)
        source = partial.at[ring_column(place - ways[k % 2], count), :, lanes]
        copies.append(ring_copy(0, k, source))
        copies[k].start()
    sent = list(copies)
    for step in range(count - 1):
        for k in range(streams):
            lanes = pl.ds(k * size, size)
            copies[k].wait_recv()
            mine = partial[ring_column(place - ways[k % 2] * (step + 2), count), :, lanes]
            value = landed[k, step].astype(jnp.float32) + mine.astype(jnp.float32)
            value = value.astype(jnp.bfloat16)
            if step < count - 2:
                running[k, step] = value
                copies[k] = ring_copy(step + 1, k, running.at[k, step])
                copies[k].start()
                sent.append(copies[k])
            else:
                share_ref[:, lanes] = value
    for copy in sent:
        copy.wait_send()


def summed_share(base, count, wide):
    block, width = base.shape
    strip = block // count
    chunks = block // LANES
    streams = 4
    piece = wide * LANES // streams
    vmem = pl.BlockSpec(memory_space=pltpu.VMEM)
    return pl.pallas_call(
        functools.partial(share_kernel, count, wide),
        out_shape=(
            jax.ShapeDtypeStruct((strip, wide * LANES), jnp.bfloat16),
            jax.ShapeDtypeStruct((width // 4, 4 * block), jnp.bfloat16),
        ),
        in_specs=[pl.BlockSpec(memory_space=pl.ANY)],
        out_specs=(vmem, vmem),
        scratch_shapes=[
            pltpu.VMEM((4, chunks, LANES, width), jnp.bfloat16),
            pltpu.VMEM((count, strip, wide * LANES), jnp.bfloat16),
            pltpu.VMEM((streams, count - 1, strip, piece), jnp.bfloat16),
            pltpu.VMEM((streams, count - 1, strip, piece), jnp.bfloat16),
            pltpu.SemaphoreType.DMA((3, chunks)),
            pltpu.SemaphoreType.DMA((3, chunks)),
            pltpu.SemaphoreType.DMA,
            pltpu.SemaphoreType.DMA((streams, count - 1)),
            pltpu.SemaphoreType.DMA((streams, count - 1)),
        ],
        compiler_params=pltpu.CompilerParams(
            collective_id=1, has_side_effects=True, vmem_limit_bytes=48 * 1024 * 1024
        ),
        name="summed_share",
    )(base.reshape(chunks, LANES, width))


def gather_plan(count):
    hops = (count // 2, count - 1 - count // 2)
    ring = [(w, s) for s in range(1, hops[0] + 1) for w in (0, 1) if s <= hops[w]]
    order = []
    first = [("a",) + hop for hop in ring]
    second = [("b", x) + hop for hop in ring for x in (0, 1)]
    second.sort(key=lambda m: (m[3], m[1], m[2]))
    third = [("ya", 0, 0)] + [("ya",) + hop for hop in ring]
    order += [first[0], first[1], ("start_b",), ("yb",), third[0]]
    order += [first[2], first[3], third[1]]
    rest = first[4:]
    tail = []
    index = 2
    while second or rest:
        for source, amount in ((rest, 2), (second, 2)):
            for _ in range(amount):
                if source:
                    tail.append(source.pop(0))
        if index < len(third):
            tail.append(third[index])
            index += 1
    tail += third[index:]
    return hops, order + tail


def gather_names(count):
    _, order = gather_plan(count)
    arrivals = [m for m in order if m[0] != "start_b"]
    partner = [("p",) + m for m in arrivals] + [("p", "own_a"), ("p", "own_b")]
    return {name: number for number, name in enumerate(arrivals + partner)}


def gather_steps(count, head, land, send_sems, recv_sems):
    me, column = lax.axis_index("row"), lax.axis_index("col")
    place = ring_place(column, count)
    sign = 1 - 2 * lax.rem(me, 2)
    ways = (sign, -sign)
    (long, short), order = gather_plan(count)
    hops = (long, short)
    names = gather_names(count)
    strip = land.shape[1]
    rows = {"a": pl.ds(0, head), "b": pl.ds(head, strip - head)}

    def where(name, mirrored=False):
        kind = name[0]
        if kind == "p":
            return where(name[1:], True)
        w, s, bits, part = 0, 0, 0, kind[-1]
        if kind in ("a", "ya"):
            w, s = name[1], name[2]
            bits = 2 if kind == "ya" else 0
        elif kind == "b":
            bits, w, s = 2 * name[1], name[2], name[3]
        elif kind == "yb":
            bits = 2
        if mirrored:
            bits = bits + 1
        way = -ways[w] if mirrored else ways[w]
        owner = flipped(me, bits) * count + ring_column(place - way * s, count)
        return land.at[owner, rows[part]]

    def target(name):
        if name[0] == "p":
            return {"row": flipped(me, 1)}
        if name[0] in ("ya", "yb"):
            return {"row": flipped(me, 2)}
        w = name[1] if name[0] == "a" else name[2]
        return {"col": ring_column(place + ways[w], count)}

    def copy_of(name, source):
        number = names[name]
        return remote(source, source, send_sems.at[number], recv_sems.at[number], target(name))

    sent = []

    def send(name, held):
        copy = copy_of(name, held)
        copy.start()
        sent.append(copy)

    own_a, own_b = where(("own_a",)), where(("own_b",))

    def begin():
        send(("a", 0, 1), own_a)
        send(("a", 1, 1), own_a)
        send(("yb",), own_b)
        send(("ya", 0, 0), own_a)
        send(("p", "own_a"), own_a)
        send(("p", "own_b"), own_b)

    def arrive(name):
        held = where(name)
        copy_of(name, held).wait_recv()
        if name[0] == "a":
            w, s = name[1:]
            if s < hops[w]:
                send(("a", w, s + 1), held)
            send(("ya", w, s), held)
        elif name[0] == "b":
            x, w, s = name[1:]
            if s < hops[w]:
                send(("b", x, w, s + 1), held)
        elif name[0] == "yb":
            send(("b", 1, 0, 1), held)
            send(("b", 1, 1, 1), held)
        send(("p",) + name, held)

    def step_of(name):
        if name[0] == "start_b":
            def start_b():
                send(("b", 0, 0, 1), own_b)
                send(("b", 0, 1, 1), own_b)

            return start_b
        return functools.partial(arrive, name)

    def finish():
        for name in names:
            if name[0] == "p":
                held = where(name)
                copy_of(name, held).wait_recv()
        for name in names:
            copy_of(name, own_a if rows_of(name) == "a" else own_b).wait_send()

    def rows_of(name):
        kind = name[1] if name[0] == "p" else name[0]
        return kind[-1]

    return begin, [step_of(name) for name in order], finish


def update_kernel(
    count, factor, head, share_ref, slab_ref, out_ref, gram, land, first, rough, exact,
    stage, sends, recvs, own_sem, free_sem, out_send, out_recv,
):
    size = gram.shape[0]
    blocks = size // LANES
    strip, reach = land.shape[1:]
    wide = reach // LANES
    width = slab_ref.shape[0]
    tile = 512 if size % 512 == 0 else LANES
    block = size // 4
    me, column = lax.axis_index("row"), lax.axis_index("col")
    place = ring_place(column, count)
    number = me * count + column
    ring = [{"col": ring_column(place + way, count)} for way in (1, -1)]
    near = ring + [{"row": flipped(me, bits)} for bits in (1, 2)]
    meet(pltpu.get_barrier_semaphore(), near + [{"row": flipped(me, 3)}])

    def begin_of(strip_number):
        return lax.div(strip_number * strip, LANES)

    def column_block(index):
        return pl.ds(pl.multiple_of(lax.rem(index, blocks) * LANES, LANES), LANES)

    def row_strip(strip_number):
        return pl.ds(pl.multiple_of(strip_number * strip, 16), strip)

    def assemble():
        @pl.loop(0, land.shape[0])
        def _(k):
            base = begin_of(k)
            for t in range(wide):
                gram[row_strip(k), column_block(base + t)] = land[
                    k, :, t * LANES : (t + 1) * LANES
                ]

        def body(i, carry):
            single, double = carry
            here = column_block(i)

            def squares(total, piece):
                value = piece.astype(jnp.float32)
                return total + jnp.sum(value * value, axis=0, keepdims=True)

            single = squares(single, gram[here, here])
            for d in range(1, blocks // 2):
                there = column_block(i + d)
                piece = gram[here, there]
                gram[there, here] = piece.T
                double = squares(double, piece)
            single = squares(single, gram[here, column_block(i + blocks // 2)])
            return single, double

        zero = jnp.zeros((1, LANES), jnp.float32)
        single, double = lax.fori_loop(0, blocks, body, (zero, zero))
        return jnp.sum(single + 2.0 * double, axis=1, keepdims=True)

    own = pltpu.make_async_copy(share_ref, land.at[number], own_sem)
    own.start()
    own.wait()
    begin, steps, finish = gather_steps(count, head, land, sends.at[0], recvs.at[0])
    begin()
    for step in steps:
        step()
    finish()
    quartic = assemble()
    for target in near:
        pl.semaphore_signal(
            free_sem, inc=1, device_id=target, device_id_type=pl.DeviceIdType.MESH
        )
    scale = 1.0 / jnp.sqrt(jnp.sqrt(quartic) + EPSILON)
    square = scale * scale

    def times_gram(source, finish, hooks=()):
        @pl.loop(0, size // tile)
        def _(step):
            for k, calls in enumerate(hooks):
                if calls:
                    @pl.when(step == k)
                    def _():
                        for call in calls:
                            call()

            columns = pl.ds(pl.multiple_of(step * tile, tile), tile)
            finish(
                columns,
                jnp.dot(source[...], gram[:, columns], preferred_element_type=jnp.float32),
            )

    part = exact.at[pl.ds(0, strip)]
    left, right = rough.at[pl.ds(0, strip)], first.at[pl.ds(0, strip)]
    mine = gram.at[row_strip(number)]

    def after_square(columns, value):
        value = value * square * square
        part[:, columns] = (
            COEF_LINEAR * (mine[:, columns].astype(jnp.float32) * square)
            + COEF_CUBIC * value
        )
        left[:, columns] = value.astype(jnp.bfloat16)

    def after_cube(columns, value):
        right[:, columns] = (
            part[:, columns] + COEF_QUINTIC * (value * square)
        ).astype(jnp.bfloat16)

    def after_third(columns, value):
        value = value * square
        part[:, columns] = (
            COEF_LINEAR * right[:, columns].astype(jnp.float32) + COEF_CUBIC * value
        )
        left[:, columns] = value.astype(jnp.bfloat16)

    def after_fourth(columns, value):
        right[:, columns] = (
            part[:, columns] + COEF_QUINTIC * (value * square)
        ).astype(jnp.bfloat16)

    times_gram(mine, after_square)
    times_gram(left, after_cube)
    times_gram(right, after_third)
    times_gram(left, after_fourth)

    pl.semaphore_wait(free_sem, len(near))
    base = begin_of(number)
    for t in range(wide):
        land[number, :, t * LANES : (t + 1) * LANES] = right[:, column_block(base + t)]

    begin, steps, finish = gather_steps(count, head, land, sends.at[1], recvs.at[1])
    begin()
    slots = size // tile
    paced = [[] for _ in range(2 * slots)]
    for k, step in enumerate(steps):
        paced[min(2 * slots - 1, k * 5 // 6)].append(step) if k * 5 // 6 < 2 * slots else None
    early = sum(len(calls) for calls in paced)

    def keep(columns, value):
        value = value * square
        exact[:, columns] = (
            COEF_LINEAR * slab_ref[:, columns].astype(jnp.float32) + COEF_CUBIC * value
        )
        rough[:, columns] = value.astype(jnp.bfloat16)

    def combine(columns, value):
        first[:, columns] = (
            exact[:, columns] + COEF_QUINTIC * (value * square)
        ).astype(jnp.bfloat16)

    times_gram(slab_ref, keep, paced[:slots])
    times_gram(rough, combine, paced[slots:])
    for step in steps[early:]:
        step()
    finish()
    assemble()

    def after_product(columns, value):
        exact[:, columns] = (
            COEF_LINEAR * first[:, columns].astype(jnp.float32) + COEF_CUBIC * value
        )
        rough[:, columns] = value.astype(jnp.bfloat16)

    times_gram(first, after_product)

    lanes = pl.ds(pl.multiple_of(me * width, LANES), width)

    def out_copy(bits):
        return remote(
            stage.at[bits],
            out_ref.at[:, lanes],
            out_send.at[bits - 1],
            out_recv.at[bits - 1],
            {"row": flipped(me, bits)},
        )

    @pl.loop(0, 4)
    def _(step):
        bits = 3 - step
        chip, core = lax.div(me, 2), lax.rem(me, 2)
        high, low = lax.div(bits, 2), lax.rem(bits, 2)
        owner = 2 * (chip + high - 2 * chip * high) + (core + low - 2 * core * low)
        columns = pl.ds(pl.multiple_of(owner * block, LANES), block)
        value = jnp.dot(rough[...], gram[:, columns], preferred_element_type=jnp.float32)
        value = (exact[:, columns] + COEF_QUINTIC * value) * (scale * factor)
        stage[bits] = value.astype(jnp.bfloat16).T
        for x in range(1, 4):
            @pl.when(bits == x)
            def _():
                out_copy(x).start()

    kept = pltpu.make_async_copy(stage.at[0], out_ref.at[:, lanes], own_sem)
    kept.start()
    kept.wait()
    for bits in range(1, 4):
        out_copy(bits).wait()


def updated(share, slab, factor, count, wide):
    width, size = slab.shape
    strip = share.shape[0]
    head = strip * 4 // 7 // 16 * 16
    vmem = pl.BlockSpec(memory_space=pltpu.VMEM)
    half = pltpu.VMEM((width, size), jnp.bfloat16)
    messages = len(gather_names(count))
    return pl.pallas_call(
        functools.partial(update_kernel, count, factor, head),
        out_shape=jax.ShapeDtypeStruct((size // 4, 4 * width), jnp.bfloat16),
        in_specs=[vmem, vmem],
        out_specs=pl.BlockSpec(memory_space=pl.ANY),
        scratch_shapes=[
            pltpu.VMEM((size, size), jnp.bfloat16),
            pltpu.VMEM((4 * count, strip, wide * LANES), jnp.bfloat16),
            half,
            half,
            pltpu.VMEM((width, size), jnp.float32),
            pltpu.VMEM((4, size // 4, width), jnp.bfloat16),
            pltpu.SemaphoreType.DMA((2, messages)),
            pltpu.SemaphoreType.DMA((2, messages)),
            pltpu.SemaphoreType.DMA,
            pltpu.SemaphoreType.REGULAR,
            pltpu.SemaphoreType.DMA((3,)),
            pltpu.SemaphoreType.DMA((3,)),
        ],
        compiler_params=pltpu.CompilerParams(
            collective_id=2, has_side_effects=True, vmem_limit_bytes=63 * 1024 * 1024
        ),
        name="updated",
    )(share, slab)


def per_device(factor, gradient, momentum):
    rows = lax.axis_size("row")
    grad32 = gradient.astype(jnp.float32)
    buffer = MOMENTUM_DECAY * momentum + grad32
    nesterov = grad32 + MOMENTUM_DECAY * buffer
    base = nesterov.astype(jnp.bfloat16)
    block = base.shape[0]
    count = lax.axis_size("col")
    strip = block // count
    if (
        rows == 4
        and count % 2 == 0
        and count >= 4
        and block % LANES == 0
        and base.shape[1] % (4 * LANES) == 0
        and strip * count == block
        and strip % 16 == 0
        and 32 <= strip <= LANES
    ):
        wide = 4 * block // LANES // 2 + 2
        share, slab = summed_share(base, count, wide)
        return (updated(share, slab, factor, count, wide), buffer)
    half = block // 2
    middle = rows // 2
    me = lax.axis_index("row")
    panel = lax.all_gather(base, "row", axis=0, tiled=True)

    def rows_of(offset):
        start = ((me + offset) % rows) * block
        return lax.dynamic_slice_in_dim(panel, start, block, axis=0)

    parts = [outer_rows(base, base)]
    for offset in range(1, middle):
        parts.append(outer_rows(rows_of(offset), base))
    facing = rows_of(middle)
    lower = me < middle
    parts.append(
        outer_rows(
            jnp.where(lower, base[:half], facing[half:]), jnp.where(lower, facing, base)
        )
    )
    partial_value = jnp.concatenate([part.astype(jnp.bfloat16) for part in parts], axis=0)
    count = lax.axis_size("col")
    if block % 128 or count % 2 or count < 4:
        share = lax.psum_scatter(partial_value, "col", scatter_dimension=0, tiled=True)
    else:
        share = ring_sum(partial_value, count)
    shares = lax.all_gather(share, ("row", "col"), axis=0, tiled=True)
    parts = rows
    if block % 128:
        shares = assembled(shares.reshape(rows, -1, block), rows, block)
        parts = 1

    width = panel.shape[1] // rows
    slab = lax.dynamic_slice_in_dim(panel, me * width, width, axis=1)
    update = chain(shares, slab, factor, parts)
    update = lax.all_to_all(update, "row", 0, 1, tiled=True)
    return (update, buffer)


def solution(mesh):
    def whole(gradient, momentum):
        factor = 0.2 * math.sqrt(max(gradient.shape))
        return jax.shard_map(
            functools.partial(per_device, factor),
            mesh=mesh,
            in_specs=(P("row", "col"), P("row", "col")),
            out_specs=(P("row", "col"), P("row", "col")),
            check_vma=False,
        )(gradient, momentum)

    return whole
```

```python
import functools
import math

import jax
import jax.numpy as jnp
from jax import lax
from jax.experimental import pallas as pl
from jax.experimental.pallas import tpu as pltpu
from jax.sharding import PartitionSpec as P

ITERS = 2

MOMENTUM_DECAY = 0.95
EPSILON = 1e-07
COEF_LINEAR = 3.4445
COEF_CUBIC = -4.775
COEF_QUINTIC = 2.0315


def outer_rows(left, right):
    return lax.dot_general(
        left, right, (((1,), (1,)), ((), ())), preferred_element_type=jnp.float32
    )


def direct_blocks(rows, block):
    if rows == 1:
        return [(0, 0, block, 0, 0)]
    half = block // 2
    middle = rows // 2
    found = []
    for j in range(rows):
        for offset in range(middle):
            i = (j + offset) % rows
            found.append((j, offset * block, block, i * block, j * block))
        low, high = min(j, (j + middle) % rows), max(j, (j + middle) % rows)
        top = low * block + (0 if j == low else half)
        found.append((j, middle * block, half, top, high * block))
    return found


def mirrored_blocks(rows):
    if rows == 1:
        return []
    middle = rows // 2
    pairs = [((j + k) % rows, j) for j in range(rows) for k in range(1, middle)]
    return pairs + [(low, low + middle) for low in range(middle)]


def chain_kernel(
    tile, factor, rows, shares_ref, x_ref, out_ref, gram_ref, first, one, two, rough, exact, total, sems
):
    size = gram_ref.shape[0]
    block = size // rows
    stride = shares_ref.shape[0] // rows
    strip = 128
    copies = []
    for number, (owner, start, height, row, column) in enumerate(direct_blocks(rows, block)):
        copies.append(
            pltpu.make_async_copy(
                shares_ref.at[pl.ds(owner * stride + start, height), :],
                gram_ref.at[pl.ds(row, height), pl.ds(column, block)],
                sems.at[number],
            )
        )
    for copy in copies:
        copy.start()
    for copy in copies:
        copy.wait()

    def squares(i, j, mirror):
        def body(step, carry):
            lanes = pl.ds(pl.multiple_of(j * block + step * strip, strip), strip)
            piece = gram_ref[pl.ds(i * block, block), lanes]
            if mirror:
                gram_ref[lanes, pl.ds(i * block, block)] = piece.T
            wide = piece.astype(jnp.float32)
            return carry + jnp.sum(wide * wide, axis=0, keepdims=True)

        return lax.fori_loop(0, block // strip, body, jnp.zeros((1, strip), jnp.float32))

    diagonal = sum(squares(i, i, False) for i in range(rows))
    others = sum(squares(i, j, True) for i, j in mirrored_blocks(rows)) + jnp.zeros_like(diagonal)
    quartic = jnp.sum(diagonal + 2.0 * others, axis=1, keepdims=True)
    scale = 1.0 / jnp.sqrt(jnp.sqrt(quartic) + EPSILON)
    square = scale * scale

    def times_gram(source, finish):
        @pl.loop(0, size // tile)
        def _(step):
            columns = pl.ds(pl.multiple_of(step * tile, tile), tile)
            value = jnp.dot(
                source[...], gram_ref[:, columns], preferred_element_type=jnp.float32
            )
            finish(columns, value * square)

    def polynomial(source, target):
        def keep(columns, value):
            exact[:, columns] = value
            rough[:, columns] = value.astype(jnp.bfloat16)

        def combine(columns, value):
            target[:, columns] = (
                COEF_LINEAR * source[:, columns].astype(jnp.float32)
                + COEF_CUBIC * exact[:, columns]
                + COEF_QUINTIC * value
            ).astype(jnp.bfloat16)

        times_gram(source, keep)
        times_gram(rough, combine)

    width = x_ref.shape[1]
    lanes_step = 128 if width % 128 == 0 else width

    @pl.loop(0, size // strip)
    def _(step):
        chunk = pl.ds(pl.multiple_of(step * strip, strip), strip)
        for lane in range(0, width, lanes_step):
            two[lane : lane + lanes_step, chunk] = x_ref[chunk, lane : lane + lanes_step].T

    polynomial(two, first)
    polynomial(first, one)
    polynomial(one, two)

    def after_product(columns, value):
        total[:, columns] = (
            COEF_LINEAR * first[:, columns].astype(jnp.float32) + COEF_CUBIC * value
        )
        one[:, columns] = value.astype(jnp.bfloat16)

    times_gram(two, after_product)
    polynomial(one, two)
    polynomial(two, one)

    def after_second(columns, value):
        two[:, columns] = (
            (total[:, columns] + COEF_QUINTIC * value) * (scale * factor)
        ).astype(jnp.bfloat16)

    times_gram(one, after_second)

    @pl.loop(0, size // strip)
    def _(step):
        chunk = pl.ds(pl.multiple_of(step * strip, strip), strip)
        for lane in range(0, width, lanes_step):
            out_ref[chunk, lane : lane + lanes_step] = two[lane : lane + lanes_step, chunk].T


def chain(shares, slab, factor, rows):
    size, width = slab.shape
    tile = 512 if size % 512 == 0 else size
    vmem = pl.BlockSpec(memory_space=pltpu.VMEM)
    half = pltpu.VMEM((width, size), jnp.bfloat16)
    full = pltpu.VMEM((width, size), jnp.float32)
    count = rows * (rows // 2 + 1)
    return pl.pallas_call(
        functools.partial(chain_kernel, tile, factor, rows),
        out_shape=jax.ShapeDtypeStruct((size, width), jnp.bfloat16),
        in_specs=[pl.BlockSpec(memory_space=pl.ANY), vmem],
        out_specs=vmem,
        scratch_shapes=[pltpu.VMEM((size, size), jnp.bfloat16)]
        + [half, half, half, half, full, full, pltpu.SemaphoreType.DMA((count,))],
        compiler_params=pltpu.CompilerParams(vmem_limit_bytes=63 * 1024 * 1024),
        name="chain",
    )(shares, slab)


def assembled(shares, rows, block):
    half = block // 2
    middle = rows // 2

    def at(i, j):
        offset = (i - j) % rows
        if offset < middle:
            return shares[j, offset * block : (offset + 1) * block]
        if offset > middle:
            return at(j, i).T
        low, high = min(i, j), max(i, j)
        value = jnp.concatenate([shares[low, -half:], shares[high, -half:]], axis=0)
        return value if i == low else value.T

    return jnp.concatenate(
        [
            jnp.concatenate([at(i, j) for j in range(rows)], axis=1)
            for i in range(rows)
        ],
        axis=0,
    )


def ring_kernel(partial_ref, out_ref, *scratch):
    landed, running, send_sems, recv_sems = scratch[:2], scratch[2:4], scratch[4], scratch[5]
    count = partial_ref.shape[0]
    column = lax.axis_index("col")
    odd, pair = lax.rem(column, 2), lax.div(column, 2)
    place = (1 - odd) * pair + odd * (count - 1 - pair)
    sign = 1 - 2 * lax.rem(lax.axis_index("row"), 2)
    ways = (sign, -sign)
    wide = landed[0].shape[2]
    lanes = (pl.ds(0, wide), pl.ds(wide, landed[1].shape[2]))

    def column_at(spot):
        spot = lax.rem(spot + 2 * count, count)
        back = lax.div(spot, count // 2)
        return (1 - back) * 2 * spot + back * (2 * (count - 1 - spot) + 1)

    barrier = pltpu.get_barrier_semaphore()
    for way in ways:
        pl.semaphore_signal(
            barrier,
            inc=1,
            device_id={"col": column_at(place + way)},
            device_id_type=pl.DeviceIdType.MESH,
        )
    pl.semaphore_wait(barrier, 2)

    def copy_of(step, k, source):
        return pltpu.make_async_remote_copy(
            src_ref=source,
            dst_ref=landed[k].at[step],
            send_sem=send_sems.at[k, step],
            recv_sem=recv_sems.at[k, step],
            device_id={"col": column_at(place + ways[k])},
            device_id_type=pl.DeviceIdType.MESH,
        )

    copies = []
    for k in range(2):
        source = partial_ref.at[column_at(place - ways[k]), :, lanes[k]]
        copies.append([copy_of(0, k, source)])
        copies[k][0].start()
    for step in range(count - 1):
        for k in range(2):
            copies[k][step].wait_recv()
            mine = partial_ref[column_at(place - ways[k] * (step + 2)), :, lanes[k]]
            value = landed[k][step].astype(jnp.float32) + mine.astype(jnp.float32)
            value = value.astype(jnp.bfloat16)
            if step < count - 2:
                running[k][step] = value
                copies[k].append(copy_of(step + 1, k, running[k].at[step]))
                copies[k][step + 1].start()
            else:
                out_ref[:, lanes[k]] = value
    for k in range(2):
        for copy in copies[k]:
            copy.wait_send()


def ring_sum(partial_value, count):
    block = partial_value.shape[1]
    height = partial_value.shape[0] // count
    wide = (block // 128 + 1) // 2 * 128
    vmem = pl.BlockSpec(memory_space=pltpu.VMEM)
    slots = [
        pltpu.VMEM((count - 1, height, width), jnp.bfloat16) for width in (wide, block - wide)
    ]
    sems = pltpu.SemaphoreType.DMA((2, count - 1))
    return pl.pallas_call(
        ring_kernel,
        out_shape=jax.ShapeDtypeStruct((height, block), jnp.bfloat16),
        in_specs=[vmem],
        out_specs=vmem,
        scratch_shapes=slots + slots + [sems, sems],
        compiler_params=pltpu.CompilerParams(
            collective_id=0, has_side_effects=True, vmem_limit_bytes=40 * 1024 * 1024
        ),
        name="ring_sum",
    )(partial_value.reshape(count, height, block))


LANES = 128


def ring_place(column, count):
    odd, pair = lax.rem(column, 2), lax.div(column, 2)
    return (1 - odd) * pair + odd * (count - 1 - pair)


def ring_column(spot, count):
    spot = lax.rem(spot + 2 * count, count)
    back = lax.div(spot, count // 2)
    return (1 - back) * 2 * spot + back * (2 * (count - 1 - spot) + 1)


def flipped(row, bits):
    chip, core = lax.div(row, 2), lax.rem(row, 2)
    if bits & 2:
        chip = 1 - chip
    if bits & 1:
        core = 1 - core
    return 2 * chip + core


def meet(barrier, targets):
    for target in targets:
        pl.semaphore_signal(
            barrier, inc=1, device_id=target, device_id_type=pl.DeviceIdType.MESH
        )
    pl.semaphore_wait(barrier, len(targets))


def remote(source, target, send_sem, recv_sem, device):
    return pltpu.make_async_remote_copy(
        src_ref=source,
        dst_ref=target,
        send_sem=send_sem,
        recv_sem=recv_sem,
        device_id=device,
        device_id_type=pl.DeviceIdType.MESH,
    )


def share_kernel(
    count, wide, base_ref, share_ref, slab_ref, panel, partial, landed, running,
    panel_send, panel_recv, own_sem, ring_send, ring_recv,
):
    chunks = panel.shape[1]
    block = chunks * LANES
    strip = block // count
    width = panel.shape[3] // 4
    me, column = lax.axis_index("row"), lax.axis_index("col")
    core = lax.rem(me, 2)
    place = ring_place(column, count)
    sign = 1 - 2 * core
    ways = (sign, -sign)
    meet(
        pltpu.get_barrier_semaphore(),
        [{"col": ring_column(place + way, count)} for way in ways]
        + [{"row": flipped(me, 1)}, {"row": flipped(me, 2)}],
    )

    def pass_on(slot, source, chunk):
        return remote(
            source,
            panel.at[slot, chunk],
            panel_send.at[slot - 1, chunk],
            panel_recv.at[slot - 1, chunk],
            {"row": flipped(me, 2 if slot == 2 else 1)},
        )

    own = pltpu.make_async_copy(base_ref, panel.at[0], own_sem)
    own.start()
    for chunk in range(chunks):
        pass_on(2, base_ref.at[chunk], chunk).start()
        pass_on(1, base_ref.at[chunk], chunk).start()
    own.wait()

    @pl.loop(0, 4 * chunks)
    def _(event):
        far = event >= 2 * chunks
        late = lax.max(event - 2 * chunks, 0)
        slot = jnp.where(far, 2 + lax.rem(late, 2), lax.div(event, chunks))
        chunk = jnp.where(far, lax.div(late, 2), lax.rem(event, chunks))
        for x in range(1, 4):
            @pl.when(slot == x)
            def _():
                pass_on(x, panel.at[2 if x == 3 else 0, chunk], chunk).wait_recv()
                if x == 2:
                    pass_on(3, panel.at[2, chunk], chunk).start()

        turned = lax.rem(slot, 2)
        offset = jnp.where(
            slot == 2, 2, turned * (2 - (1 - 2 * core) * (2 - slot))
        )
        owner = lax.rem(me + offset, 4)
        piece = panel[slot, chunk]
        target = pl.ds(pl.multiple_of((owner * chunks + chunk) * LANES, LANES), LANES)
        mine = pl.ds(pl.multiple_of(me * width, LANES), width)
        slab_ref[:, target] = panel[slot, chunk, :, mine].T
        spot = offset * chunks + chunk

        @pl.when(spot < chunks + wide - 1)
        def _():
            value = outer_rows(panel[0].reshape(block, panel.shape[3]), piece)
            value = value.astype(jnp.bfloat16)
            for i in range(chunks):
                place_in = spot - i

                @pl.when((place_in >= 0) & (place_in < wide))
                def _():
                    lanes = pl.ds(pl.multiple_of(place_in * LANES, LANES), LANES)
                    held = slice(i * LANES, (i + 1) * LANES)
                    partial[held, lanes] = value[held]

    for slot in range(1, 4):
        for chunk in range(chunks):
            pass_on(slot, panel.at[2 if slot == 3 else 0, chunk], chunk).wait_send()

    size = landed.shape[3]
    lanes = [
        pl.ds(start, min(size, wide * LANES - start))
        for start in range(0, wide * LANES, size)
    ]

    def strip_at(spot):
        spot = lax.rem(spot + 2 * count, count)
        return pl.ds(pl.multiple_of(spot * strip, 16), strip)

    def ring_copy(step, k, source):
        return remote(
            source,
            landed.at[k, step, :, pl.ds(0, lanes[k].size)],
            ring_send.at[k, step],
            ring_recv.at[k, step],
            {"col": ring_column(place + ways[k % 2], count)},
        )

    copies = []
    for k in range(len(lanes)):
        source = partial.at[strip_at(place - ways[k % 2]), lanes[k]]
        copies.append(ring_copy(0, k, source))
        copies[k].start()
    sent = list(copies)
    for step in range(count - 1):
        for k in range(len(lanes)):
            held = pl.ds(0, lanes[k].size)
            copies[k].wait_recv()
            mine = partial[strip_at(place - ways[k % 2] * (step + 2)), lanes[k]]
            value = landed[k, step, :, held].astype(jnp.float32) + mine.astype(jnp.float32)
            value = value.astype(jnp.bfloat16)
            if step < count - 2:
                running[k, step, :, held] = value
                copies[k] = ring_copy(step + 1, k, running.at[k, step, :, held])
                copies[k].start()
                sent.append(copies[k])
            else:
                share_ref[:, lanes[k]] = value
    for copy in sent:
        copy.wait_send()


def summed_share(base, count, wide):
    block, width = base.shape
    strip = block // count
    chunks = block // LANES
    streams = 4
    piece = pl.cdiv(wide, streams) * LANES
    vmem = pl.BlockSpec(memory_space=pltpu.VMEM)
    return pl.pallas_call(
        functools.partial(share_kernel, count, wide),
        out_shape=(
            jax.ShapeDtypeStruct((strip, wide * LANES), jnp.bfloat16),
            jax.ShapeDtypeStruct((width // 4, 4 * block), jnp.bfloat16),
        ),
        in_specs=[pl.BlockSpec(memory_space=pl.ANY)],
        out_specs=(vmem, vmem),
        scratch_shapes=[
            pltpu.VMEM((4, chunks, LANES, width), jnp.bfloat16),
            pltpu.VMEM((block, wide * LANES), jnp.bfloat16),
            pltpu.VMEM((streams, count - 1, strip, piece), jnp.bfloat16),
            pltpu.VMEM((streams, count - 1, strip, piece), jnp.bfloat16),
            pltpu.SemaphoreType.DMA((3, chunks)),
            pltpu.SemaphoreType.DMA((3, chunks)),
            pltpu.SemaphoreType.DMA,
            pltpu.SemaphoreType.DMA((streams, count - 1)),
            pltpu.SemaphoreType.DMA((streams, count - 1)),
        ],
        compiler_params=pltpu.CompilerParams(
            collective_id=1, has_side_effects=True, vmem_limit_bytes=48 * 1024 * 1024
        ),
        name="summed_share",
    )(base.reshape(chunks, LANES, width))


def gather_plan(count):
    hops = (count // 2, count - 1 - count // 2)
    ring = [(w, s) for s in range(1, hops[0] + 1) for w in (0, 1) if s <= hops[w]]
    first = [("a",) + hop for hop in ring]
    second = [("b", x) + hop for hop in ring for x in (0, 1)]
    second.sort(key=lambda m: (m[3], m[1], m[2]))
    third = [("ya", 0, 0)] + [("ya",) + hop for hop in ring]
    order = [first[0], first[1], ("start_b",), ("yb",), third[0]]
    order += [first[2], first[3], third[1]]
    rest = first[4:]
    index = 2
    while second or rest:
        for source in (rest, second):
            order += source[:2]
            del source[:2]
        order += third[index : index + 1]
        index += 1
    return hops, order + third[index:]


def gather_names(count):
    _, order = gather_plan(count)
    arrivals = [m for m in order if m[0] != "start_b"]
    partner = [("p",) + m for m in arrivals] + [("p", "own_a"), ("p", "own_b")]
    return {name: number for number, name in enumerate(arrivals + partner)}


def strip_names(bits, u):
    if u == 0:
        near = [[], [("ya", 0, 0), ("yb",)]][bits // 2]
        if bits == 1:
            return [("p", "own_a"), ("p", "own_b")]
    else:
        w, s = (0, -u) if u < 0 else (1, u)
        near = [("ya" if bits & 2 else "a", w, s), ("b", bits // 2, w, s)]
    return [("p",) + m for m in near] if bits & 1 else near


def gather_groups(count, width):
    (long, short), order = gather_plan(count)
    works = []
    for bits in range(4):
        for u in range(-long, short + 1):
            after = u + 1 if u < short else -long
            works.append((bits, u, strip_names(bits, u) + strip_names(bits, after)))
    seen = set()
    groups = []
    for start in range(0, len(order), width):
        events = order[start : start + width]
        due = set(seen)
        seen.update(events)
        ready = []
        for work in list(works):
            names = [m[1:] if m[0] == "p" else m for m in work[2]]
            known = due if work[0] & 1 else seen
            if all(m in known or m[0] in ("own_a", "own_b") for m in names):
                works.remove(work)
                ready.append(work)
        groups.append((events, ready))
    groups.append(([], works))
    return groups


def gather_steps(count, head, strip, land, send_sems, recv_sems):
    me, column = lax.axis_index("row"), lax.axis_index("col")
    place = ring_place(column, count)
    sign = 1 - 2 * lax.rem(me, 2)
    ways = (sign, -sign)
    hops, _ = gather_plan(count)
    names = gather_names(count)

    def where(name, mirrored=False):
        kind = name[0]
        if kind == "p":
            return where(name[1:], True)
        w, s, bits, part = 0, 0, 0, kind[-1]
        if kind in ("a", "ya"):
            w, s = name[1], name[2]
            bits = 2 if kind == "ya" else 0
        elif kind == "b":
            bits, w, s = 2 * name[1], name[2], name[3]
        elif kind == "yb":
            bits = 2
        if mirrored:
            bits = bits + 1
        way = -ways[w] if mirrored else ways[w]
        spot = lax.rem(place - way * s + count, count)
        start = (flipped(me, bits) * count + spot) * strip
        if part == "b":
            return land.at[pl.ds(pl.multiple_of(start + head, 16), strip - head)]
        return land.at[pl.ds(pl.multiple_of(start, 16), head)]

    def target(name):
        if name[0] == "p":
            return {"row": flipped(me, 1)}
        if name[0] in ("ya", "yb"):
            return {"row": flipped(me, 2)}
        w = name[1] if name[0] == "a" else name[2]
        return {"col": ring_column(place + ways[w], count)}

    def copy_of(name, source):
        number = names[name]
        return remote(source, source, send_sems.at[number], recv_sems.at[number], target(name))

    def send(name, held):
        copy_of(name, held).start()

    own_a, own_b = where(("own_a",)), where(("own_b",))

    def begin():
        send(("a", 0, 1), own_a)
        send(("a", 1, 1), own_a)
        send(("yb",), own_b)
        send(("ya", 0, 0), own_a)
        send(("p", "own_a"), own_a)
        send(("p", "own_b"), own_b)

    def arrive(name):
        if name[0] == "start_b":
            send(("b", 0, 0, 1), own_b)
            send(("b", 0, 1, 1), own_b)
            return
        held = where(name)
        copy_of(name, held).wait_recv()
        if name[0] == "a":
            w, s = name[1:]
            if s < hops[w]:
                send(("a", w, s + 1), held)
            send(("ya", w, s), held)
        elif name[0] == "b":
            x, w, s = name[1:]
            if s < hops[w]:
                send(("b", x, w, s + 1), held)
        elif name[0] == "yb":
            send(("b", 1, 0, 1), held)
            send(("b", 1, 1, 1), held)
        send(("p",) + name, held)

    def land_from_partner(name):
        copy_of(name, where(name)).wait_recv()

    def sent():
        for name in names:
            kind = name[1] if name[0] == "p" else name[0]
            copy_of(name, own_a if kind[-1] == "a" else own_b).wait_send()

    return begin, arrive, land_from_partner, sent


def update_kernel(
    count, factor, head, share_ref, slab_ref, out_ref, gram, land, first, rough, exact,
    stage, total, sends, recvs, own_sem, free_sem, out_send, out_recv,
):
    size = gram.shape[0]
    blocks = size // LANES
    strip, reach = share_ref.shape
    wide = reach // LANES
    width = slab_ref.shape[0]
    tile = 512 if size % 512 == 0 else LANES
    block = size // 4
    chunks = block // LANES
    me, column = lax.axis_index("row"), lax.axis_index("col")
    place = ring_place(column, count)
    sign = 1 - 2 * lax.rem(me, 2)
    number = me * count + place
    ring = [{"col": ring_column(place + way, count)} for way in (1, -1)]
    near = ring + [{"row": flipped(me, bits)} for bits in (1, 2)]
    meet(pltpu.get_barrier_semaphore(), near + [{"row": flipped(me, 3)}])

    def column_block(index):
        return pl.ds(pl.multiple_of(lax.rem(index, blocks) * LANES, LANES), LANES)

    mine_rows = pl.ds(pl.multiple_of(number * strip, 16), strip)

    def place_block(i, squares):
        here = column_block(i)
        single = double = jnp.zeros((8, LANES), jnp.float32)
        for d in range(wide):
            piece = land[here, d * LANES : (d + 1) * LANES]
            there = column_block(i + d)
            gram[here, there] = piece
            if 0 < d < wide - 1:
                gram[there, here] = piece.T
            if squares:
                value = piece.astype(jnp.float32)
                value = jnp.sum((value * value).reshape(LANES // 8, 8, LANES), axis=0)
                if 0 < d < wide - 1:
                    double = double + value
                else:
                    single = single + value
        if squares:
            total[...] += single + 2.0 * double

    def place_blocks(works, squares):
        if not works:
            return

        @pl.loop(0, len(works))
        def _(step):
            bits, u = works[0][:2]
            code = jnp.int32(bits * 2 * count + u + count)
            for k, (bits, u, _) in enumerate(works[1:], 1):
                code = jnp.where(step == k, bits * 2 * count + u + count, code)
            bits, u = lax.div(code, 2 * count), lax.rem(code, 2 * count) - count
            high, low = lax.div(bits, 2), lax.rem(bits, 2)
            chip, core = lax.div(me, 2), lax.rem(me, 2)
            row = 2 * (chip + high - 2 * chip * high) + (core + low - 2 * core * low)
            way = sign * (1 - 2 * low)
            spot = lax.rem(place + way * u + lax.div(way - 1, 2) + 2 * count, count)

            @pl.when(spot < chunks)
            def _():
                place_block(row * chunks + spot, squares)

    own = pltpu.make_async_copy(share_ref, land.at[mine_rows], own_sem)
    own.start()
    own.wait()
    total[...] = jnp.zeros_like(total)

    def run_groups(groups, steps, squares):
        _, arrive, land_from_partner, sent = steps
        waited = set()
        for events, works in groups:
            for name in events:
                arrive(name)
            for _, _, names in works:
                for name in names:
                    if name[0] == "p" and name not in waited:
                        waited.add(name)
                        land_from_partner(name)
            place_blocks(works, squares)
        sent()

    steps = gather_steps(count, head, strip, land, sends.at[0], recvs.at[0])
    steps[0]()
    run_groups(gather_groups(count, 4), steps, True)
    for target in near:
        pl.semaphore_signal(
            free_sem, inc=1, device_id=target, device_id_type=pl.DeviceIdType.MESH
        )
    quartic = jnp.sum(jnp.sum(total[...], axis=0, keepdims=True), axis=1, keepdims=True)
    scale = 1.0 / jnp.sqrt(jnp.sqrt(quartic) + EPSILON)
    square = scale * scale

    def times_gram(source, finish, hooks=()):
        @pl.loop(0, size // tile)
        def _(step):
            for k, calls in enumerate(hooks):
                if calls:
                    @pl.when(step == k)
                    def _():
                        for call in calls:
                            call()

            columns = pl.ds(pl.multiple_of(step * tile, tile), tile)
            finish(
                columns,
                jnp.dot(source[...], gram[:, columns], preferred_element_type=jnp.float32),
            )

    part = exact.at[pl.ds(0, strip)]
    left, right = rough.at[pl.ds(0, strip)], first.at[pl.ds(0, strip)]
    mine = gram.at[mine_rows]

    def after_square(columns, value):
        value = value * square * square
        part[:, columns] = (
            COEF_LINEAR * (mine[:, columns].astype(jnp.float32) * square)
            + COEF_CUBIC * value
        )
        left[:, columns] = value.astype(jnp.bfloat16)

    def after_cube(columns, value):
        right[:, columns] = (
            part[:, columns] + COEF_QUINTIC * (value * square)
        ).astype(jnp.bfloat16)

    def after_third(columns, value):
        value = value * square
        part[:, columns] = (
            COEF_LINEAR * right[:, columns].astype(jnp.float32) + COEF_CUBIC * value
        )
        left[:, columns] = value.astype(jnp.bfloat16)

    times_gram(mine, after_square)
    times_gram(left, after_cube)
    times_gram(right, after_third)
    times_gram(left, after_cube)

    pl.semaphore_wait(free_sem, len(near))
    for group in range(strip // 16):
        sixteenth = number * (strip // 16) + group
        base = lax.div(sixteenth, LANES // 16)
        rows = pl.ds(pl.multiple_of(sixteenth * 16, 16), 16)
        for t in range(wide):
            land[rows, t * LANES : (t + 1) * LANES] = right[
                group * 16 : group * 16 + 16, column_block(base + t)
            ]

    steps = gather_steps(count, head, strip, land, sends.at[1], recvs.at[1])
    steps[0]()
    groups = gather_groups(count, 4)
    slots = size // tile
    paced = [[] for _ in range(2 * slots)]
    early, waiting = [], []
    for k, (events, works) in enumerate(groups):
        if len(early) + len(events) <= 18:
            early += events
            waiting += works
            groups[k] = ([], [])
        else:
            groups[k] = (events, waiting + works)
            break
    for k, name in enumerate(early):
        paced[min(2 * slots - 1, k * 2 * slots // len(early))].append(
            functools.partial(steps[1], name)
        )

    def keep(columns, value):
        value = value * square
        exact[:, columns] = (
            COEF_LINEAR * slab_ref[:, columns].astype(jnp.float32) + COEF_CUBIC * value
        )
        rough[:, columns] = value.astype(jnp.bfloat16)

    def combine(columns, value):
        first[:, columns] = (
            exact[:, columns] + COEF_QUINTIC * (value * square)
        ).astype(jnp.bfloat16)

    times_gram(slab_ref, keep, paced[:slots])
    times_gram(rough, combine, paced[slots:])
    run_groups(groups, steps, False)

    def after_product(columns, value):
        exact[:, columns] = (
            COEF_LINEAR * first[:, columns].astype(jnp.float32) + COEF_CUBIC * value
        )
        rough[:, columns] = value.astype(jnp.bfloat16)

    times_gram(first, after_product)

    lanes = pl.ds(pl.multiple_of(me * width, LANES), width)

    def out_copy(bits):
        return remote(
            stage.at[bits],
            out_ref.at[:, lanes],
            out_send.at[bits - 1],
            out_recv.at[bits - 1],
            {"row": flipped(me, bits)},
        )

    @pl.loop(0, 4)
    def _(step):
        bits = 3 - step
        chip, core = lax.div(me, 2), lax.rem(me, 2)
        high, low = lax.div(bits, 2), lax.rem(bits, 2)
        owner = 2 * (chip + high - 2 * chip * high) + (core + low - 2 * core * low)
        columns = pl.ds(pl.multiple_of(owner * block, LANES), block)
        value = jnp.dot(rough[...], gram[:, columns], preferred_element_type=jnp.float32)
        value = (exact[:, columns] + COEF_QUINTIC * value) * (scale * factor)
        stage[bits] = value.astype(jnp.bfloat16).T
        for x in range(1, 4):
            @pl.when(bits == x)
            def _():
                out_copy(x).start()

    kept = pltpu.make_async_copy(stage.at[0], out_ref.at[:, lanes], own_sem)
    kept.start()
    kept.wait()
    for bits in range(1, 4):
        out_copy(bits).wait()


def updated(share, slab, factor, count, wide):
    width, size = slab.shape
    strip = share.shape[0]
    head = strip * 4 // 7 // 16 * 16
    vmem = pl.BlockSpec(memory_space=pltpu.VMEM)
    half = pltpu.VMEM((width, size), jnp.bfloat16)
    messages = len(gather_names(count))
    return pl.pallas_call(
        functools.partial(update_kernel, count, factor, head),
        out_shape=jax.ShapeDtypeStruct((size // 4, 4 * width), jnp.bfloat16),
        in_specs=[vmem, vmem],
        out_specs=pl.BlockSpec(memory_space=pl.ANY),
        scratch_shapes=[
            pltpu.VMEM((size, size), jnp.bfloat16),
            pltpu.VMEM((size, wide * LANES), jnp.bfloat16),
            half,
            half,
            pltpu.VMEM((width, size), jnp.float32),
            pltpu.VMEM((4, size // 4, width), jnp.bfloat16),
            pltpu.VMEM((8, LANES), jnp.float32),
            pltpu.SemaphoreType.DMA((2, messages)),
            pltpu.SemaphoreType.DMA((2, messages)),
            pltpu.SemaphoreType.DMA,
            pltpu.SemaphoreType.REGULAR,
            pltpu.SemaphoreType.DMA((3,)),
            pltpu.SemaphoreType.DMA((3,)),
        ],
        compiler_params=pltpu.CompilerParams(
            collective_id=2, has_side_effects=True, vmem_limit_bytes=63 * 1024 * 1024
        ),
        name="updated",
    )(share, slab)


def per_device(factor, gradient, momentum):
    rows = lax.axis_size("row")
    grad32 = gradient.astype(jnp.float32)
    buffer = MOMENTUM_DECAY * momentum + grad32
    nesterov = grad32 + MOMENTUM_DECAY * buffer
    base = nesterov.astype(jnp.bfloat16)
    block = base.shape[0]
    count = lax.axis_size("col")
    strip = block // count
    if (
        rows == 4
        and count % 2 == 0
        and count >= 4
        and block % LANES == 0
        and base.shape[1] % (4 * LANES) == 0
        and strip * count == block
        and strip % 16 == 0
        and 32 <= strip < LANES
        and block // LANES + 1 == count
    ):
        wide = 4 * block // LANES // 2 + 1
        share, slab = summed_share(base, count, wide)
        return (updated(share, slab, factor, count, wide), buffer)
    half = block // 2
    middle = rows // 2
    me = lax.axis_index("row")
    panel = lax.all_gather(base, "row", axis=0, tiled=True)

    def rows_of(offset):
        start = ((me + offset) % rows) * block
        return lax.dynamic_slice_in_dim(panel, start, block, axis=0)

    parts = [outer_rows(base, base)]
    for offset in range(1, middle):
        parts.append(outer_rows(rows_of(offset), base))
    facing = rows_of(middle)
    lower = me < middle
    parts.append(
        outer_rows(
            jnp.where(lower, base[:half], facing[half:]), jnp.where(lower, facing, base)
        )
    )
    partial_value = jnp.concatenate([part.astype(jnp.bfloat16) for part in parts], axis=0)
    count = lax.axis_size("col")
    if block % 128 or count % 2 or count < 4:
        share = lax.psum_scatter(partial_value, "col", scatter_dimension=0, tiled=True)
    else:
        share = ring_sum(partial_value, count)
    shares = lax.all_gather(share, ("row", "col"), axis=0, tiled=True)
    parts = rows
    if block % 128:
        shares = assembled(shares.reshape(rows, -1, block), rows, block)
        parts = 1

    width = panel.shape[1] // rows
    slab = lax.dynamic_slice_in_dim(panel, me * width, width, axis=1)
    update = chain(shares, slab, factor, parts)
    update = lax.all_to_all(update, "row", 0, 1, tiled=True)
    return (update, buffer)


def solution(mesh):
    def whole(gradient, momentum):
        factor = 0.2 * math.sqrt(max(gradient.shape))
        return jax.shard_map(
            functools.partial(per_device, factor),
            mesh=mesh,
            in_specs=(P("row", "col"), P("row", "col")),
            out_specs=(P("row", "col"), P("row", "col")),
            check_vma=False,
        )(gradient, momentum)

    return whole
```

```python
import functools
import math

import jax
import jax.numpy as jnp
from jax import lax
from jax.experimental import pallas as pl
from jax.experimental.pallas import tpu as pltpu
from jax.sharding import PartitionSpec as P

ITERS = 2

MOMENTUM_DECAY = 0.95
EPSILON = 1e-07
COEF_LINEAR = 3.4445
COEF_CUBIC = -4.775
COEF_QUINTIC = 2.0315


def outer_rows(left, right):
    return lax.dot_general(
        left, right, (((1,), (1,)), ((), ())), preferred_element_type=jnp.float32
    )


def direct_blocks(rows, block):
    if rows == 1:
        return [(0, 0, block, 0, 0)]
    half = block // 2
    middle = rows // 2
    found = []
    for j in range(rows):
        for offset in range(middle):
            i = (j + offset) % rows
            found.append((j, offset * block, block, i * block, j * block))
        low, high = min(j, (j + middle) % rows), max(j, (j + middle) % rows)
        top = low * block + (0 if j == low else half)
        found.append((j, middle * block, half, top, high * block))
    return found


def mirrored_blocks(rows):
    if rows == 1:
        return []
    middle = rows // 2
    pairs = [((j + k) % rows, j) for j in range(rows) for k in range(1, middle)]
    return pairs + [(low, low + middle) for low in range(middle)]


def chain_kernel(
    tile, factor, rows, shares_ref, x_ref, out_ref, gram_ref, first, one, two, rough, exact, total, sems
):
    size = gram_ref.shape[0]
    block = size // rows
    stride = shares_ref.shape[0] // rows
    strip = 128
    copies = []
    for number, (owner, start, height, row, column) in enumerate(direct_blocks(rows, block)):
        copies.append(
            pltpu.make_async_copy(
                shares_ref.at[pl.ds(owner * stride + start, height), :],
                gram_ref.at[pl.ds(row, height), pl.ds(column, block)],
                sems.at[number],
            )
        )
    for copy in copies:
        copy.start()
    for copy in copies:
        copy.wait()

    def squares(i, j, mirror):
        def body(step, carry):
            lanes = pl.ds(pl.multiple_of(j * block + step * strip, strip), strip)
            piece = gram_ref[pl.ds(i * block, block), lanes]
            if mirror:
                gram_ref[lanes, pl.ds(i * block, block)] = piece.T
            wide = piece.astype(jnp.float32)
            return carry + jnp.sum(wide * wide, axis=0, keepdims=True)

        return lax.fori_loop(0, block // strip, body, jnp.zeros((1, strip), jnp.float32))

    diagonal = sum(squares(i, i, False) for i in range(rows))
    others = sum(squares(i, j, True) for i, j in mirrored_blocks(rows)) + jnp.zeros_like(diagonal)
    quartic = jnp.sum(diagonal + 2.0 * others, axis=1, keepdims=True)
    scale = 1.0 / jnp.sqrt(jnp.sqrt(quartic) + EPSILON)
    square = scale * scale

    def times_gram(source, finish):
        @pl.loop(0, size // tile)
        def _(step):
            columns = pl.ds(pl.multiple_of(step * tile, tile), tile)
            value = jnp.dot(
                source[...], gram_ref[:, columns], preferred_element_type=jnp.float32
            )
            finish(columns, value * square)

    def polynomial(source, target):
        def keep(columns, value):
            exact[:, columns] = value
            rough[:, columns] = value.astype(jnp.bfloat16)

        def combine(columns, value):
            target[:, columns] = (
                COEF_LINEAR * source[:, columns].astype(jnp.float32)
                + COEF_CUBIC * exact[:, columns]
                + COEF_QUINTIC * value
            ).astype(jnp.bfloat16)

        times_gram(source, keep)
        times_gram(rough, combine)

    width = x_ref.shape[1]
    lanes_step = 128 if width % 128 == 0 else width

    @pl.loop(0, size // strip)
    def _(step):
        chunk = pl.ds(pl.multiple_of(step * strip, strip), strip)
        for lane in range(0, width, lanes_step):
            two[lane : lane + lanes_step, chunk] = x_ref[chunk, lane : lane + lanes_step].T

    polynomial(two, first)
    polynomial(first, one)
    polynomial(one, two)

    def after_product(columns, value):
        total[:, columns] = (
            COEF_LINEAR * first[:, columns].astype(jnp.float32) + COEF_CUBIC * value
        )
        one[:, columns] = value.astype(jnp.bfloat16)

    times_gram(two, after_product)
    polynomial(one, two)
    polynomial(two, one)

    def after_second(columns, value):
        two[:, columns] = (
            (total[:, columns] + COEF_QUINTIC * value) * (scale * factor)
        ).astype(jnp.bfloat16)

    times_gram(one, after_second)

    @pl.loop(0, size // strip)
    def _(step):
        chunk = pl.ds(pl.multiple_of(step * strip, strip), strip)
        for lane in range(0, width, lanes_step):
            out_ref[chunk, lane : lane + lanes_step] = two[lane : lane + lanes_step, chunk].T


def chain(shares, slab, factor, rows):
    size, width = slab.shape
    tile = 512 if size % 512 == 0 else size
    vmem = pl.BlockSpec(memory_space=pltpu.VMEM)
    half = pltpu.VMEM((width, size), jnp.bfloat16)
    full = pltpu.VMEM((width, size), jnp.float32)
    count = rows * (rows // 2 + 1)
    return pl.pallas_call(
        functools.partial(chain_kernel, tile, factor, rows),
        out_shape=jax.ShapeDtypeStruct((size, width), jnp.bfloat16),
        in_specs=[pl.BlockSpec(memory_space=pl.ANY), vmem],
        out_specs=vmem,
        scratch_shapes=[pltpu.VMEM((size, size), jnp.bfloat16)]
        + [half, half, half, half, full, full, pltpu.SemaphoreType.DMA((count,))],
        compiler_params=pltpu.CompilerParams(vmem_limit_bytes=63 * 1024 * 1024),
        name="chain",
    )(shares, slab)


def assembled(shares, rows, block):
    half = block // 2
    middle = rows // 2

    def at(i, j):
        offset = (i - j) % rows
        if offset < middle:
            return shares[j, offset * block : (offset + 1) * block]
        if offset > middle:
            return at(j, i).T
        low, high = min(i, j), max(i, j)
        value = jnp.concatenate([shares[low, -half:], shares[high, -half:]], axis=0)
        return value if i == low else value.T

    return jnp.concatenate(
        [
            jnp.concatenate([at(i, j) for j in range(rows)], axis=1)
            for i in range(rows)
        ],
        axis=0,
    )


def ring_kernel(partial_ref, out_ref, *scratch):
    landed, running, send_sems, recv_sems = scratch[:2], scratch[2:4], scratch[4], scratch[5]
    count = partial_ref.shape[0]
    column = lax.axis_index("col")
    odd, pair = lax.rem(column, 2), lax.div(column, 2)
    place = (1 - odd) * pair + odd * (count - 1 - pair)
    sign = 1 - 2 * lax.rem(lax.axis_index("row"), 2)
    ways = (sign, -sign)
    wide = landed[0].shape[2]
    lanes = (pl.ds(0, wide), pl.ds(wide, landed[1].shape[2]))

    def column_at(spot):
        spot = lax.rem(spot + 2 * count, count)
        back = lax.div(spot, count // 2)
        return (1 - back) * 2 * spot + back * (2 * (count - 1 - spot) + 1)

    barrier = pltpu.get_barrier_semaphore()
    for way in ways:
        pl.semaphore_signal(
            barrier,
            inc=1,
            device_id={"col": column_at(place + way)},
            device_id_type=pl.DeviceIdType.MESH,
        )
    pl.semaphore_wait(barrier, 2)

    def copy_of(step, k, source):
        return pltpu.make_async_remote_copy(
            src_ref=source,
            dst_ref=landed[k].at[step],
            send_sem=send_sems.at[k, step],
            recv_sem=recv_sems.at[k, step],
            device_id={"col": column_at(place + ways[k])},
            device_id_type=pl.DeviceIdType.MESH,
        )

    copies = []
    for k in range(2):
        source = partial_ref.at[column_at(place - ways[k]), :, lanes[k]]
        copies.append([copy_of(0, k, source)])
        copies[k][0].start()
    for step in range(count - 1):
        for k in range(2):
            copies[k][step].wait_recv()
            mine = partial_ref[column_at(place - ways[k] * (step + 2)), :, lanes[k]]
            value = landed[k][step].astype(jnp.float32) + mine.astype(jnp.float32)
            value = value.astype(jnp.bfloat16)
            if step < count - 2:
                running[k][step] = value
                copies[k].append(copy_of(step + 1, k, running[k].at[step]))
                copies[k][step + 1].start()
            else:
                out_ref[:, lanes[k]] = value
    for k in range(2):
        for copy in copies[k]:
            copy.wait_send()


def ring_sum(partial_value, count):
    block = partial_value.shape[1]
    height = partial_value.shape[0] // count
    wide = (block // 128 + 1) // 2 * 128
    vmem = pl.BlockSpec(memory_space=pltpu.VMEM)
    slots = [
        pltpu.VMEM((count - 1, height, width), jnp.bfloat16) for width in (wide, block - wide)
    ]
    sems = pltpu.SemaphoreType.DMA((2, count - 1))
    return pl.pallas_call(
        ring_kernel,
        out_shape=jax.ShapeDtypeStruct((height, block), jnp.bfloat16),
        in_specs=[vmem],
        out_specs=vmem,
        scratch_shapes=slots + slots + [sems, sems],
        compiler_params=pltpu.CompilerParams(
            collective_id=0, has_side_effects=True, vmem_limit_bytes=40 * 1024 * 1024
        ),
        name="ring_sum",
    )(partial_value.reshape(count, height, block))


LANES = 128


def ring_place(column, count):
    odd, pair = lax.rem(column, 2), lax.div(column, 2)
    return (1 - odd) * pair + odd * (count - 1 - pair)


def ring_column(spot, count):
    spot = lax.rem(spot + 2 * count, count)
    back = lax.div(spot, count // 2)
    return (1 - back) * 2 * spot + back * (2 * (count - 1 - spot) + 1)


def flipped(row, bits):
    chip, core = lax.div(row, 2), lax.rem(row, 2)
    if bits & 2:
        chip = 1 - chip
    if bits & 1:
        core = 1 - core
    return 2 * chip + core


def meet(barrier, targets):
    for target in targets:
        pl.semaphore_signal(
            barrier, inc=1, device_id=target, device_id_type=pl.DeviceIdType.MESH
        )
    pl.semaphore_wait(barrier, len(targets))


def remote(source, target, send_sem, recv_sem, device):
    return pltpu.make_async_remote_copy(
        src_ref=source,
        dst_ref=target,
        send_sem=send_sem,
        recv_sem=recv_sem,
        device_id=device,
        device_id_type=pl.DeviceIdType.MESH,
    )


def sum_share(
    count, wide, base_ref, slab, gram, partial, share, running_rows,
    panel_send, panel_recv, own_sem, ring_send, ring_recv,
):
    block, width = base_ref.shape
    chunks = block // LANES
    strip = block // count
    half = LANES // 2
    slab_width = width // 4
    me, column = lax.axis_index("row"), lax.axis_index("col")
    chip, core = lax.div(me, 2), lax.rem(me, 2)
    place = ring_place(column, count)
    sign = 1 - 2 * core
    ways = (sign, -sign)

    def panel(slot, chunk, part=None):
        start = (slot * chunks + chunk) * LANES
        if part is None:
            return gram.at[pl.ds(pl.multiple_of(start, LANES), LANES), pl.ds(0, width)]
        start = pl.multiple_of(start + part * half, half)
        return gram.at[pl.ds(start, half), pl.ds(0, width)]

    def move(kind, chunk, source, target, bits):
        return remote(
            source, target, panel_send.at[kind, chunk], panel_recv.at[kind, chunk],
            {"row": flipped(me, bits)},
        )

    def to_partner(chunk):
        rows = pl.ds(chunk * LANES, LANES)
        return move(0, chunk, base_ref.at[rows], panel(1, chunk), 1)

    def across(j, chunk, own=False):
        source = panel(1, chunk, core)
        if own:
            source = base_ref.at[pl.ds(pl.multiple_of(chunk * LANES + core * half, half), half)]
        return move(1 + j, chunk, source, panel(2 + j, chunk, core), 2)

    def beside(j, chunk, part):
        held = panel(2 + j, chunk, part)
        return move(3 + j, chunk, held, held, 1)

    own = pltpu.make_async_copy(base_ref, gram.at[pl.ds(0, block), pl.ds(0, width)], own_sem)
    own.start()
    for chunk in range(chunks):
        to_partner(chunk).start()

    for k in range(2):
        @pl.when(core == k)
        def _():
            for j in range(2):
                for chunk in range(chunks):
                    if j != k:
                        to_partner(chunk).wait_recv()
                    across(j, chunk, j == k).start()

    own.wait()
    piece = ring_send.shape[0]
    first_half = (chunks + 1) // 2 * 2 * LANES
    starts = [0, first_half // 2]
    rest = wide * LANES - first_half
    step_lanes = pl.cdiv(rest // LANES, 4) * LANES
    starts += list(range(first_half, wide * LANES, step_lanes))
    stops = starts[1:] + [wide * LANES]
    lanes = [pl.ds(start, stop - start) for start, stop in zip(starts, stops)]
    assert len(lanes) <= piece
    early, late = range(2), range(2, len(lanes))

    def strip_at(spot):
        spot = lax.rem(spot + 2 * count, count)
        return pl.ds(pl.multiple_of(spot * strip, 16), strip)

    def held_at(first, step, k):
        rows = pl.ds(pl.multiple_of(first + step * strip, 16), strip)
        return gram.at[rows, pl.ds(width + lanes[k].start, lanes[k].size)]

    def ring_copy(step, k, source):
        return remote(
            source, held_at(block, step, k), ring_send.at[k, step], ring_recv.at[k, step],
            {"col": ring_column(place + ways[k % 2], count)},
        )

    def ring_start(streams):
        for k in streams:
            ring_copy(0, k, partial.at[strip_at(place - ways[k % 2]), lanes[k]]).start()

    def ring_step(step, streams):
        for k in streams:
            landed, running = held_at(block, step, k), held_at(running_rows, step, k)
            ring_copy(step, k, landed).wait_recv()
            mine = partial[strip_at(place - ways[k % 2] * (step + 2)), lanes[k]]
            value = landed[...].astype(jnp.float32) + mine.astype(jnp.float32)
            value = value.astype(jnp.bfloat16)

            @pl.when(step < count - 2)
            def _():
                running[...] = value
                ring_copy(step + 1, k, running).start()

            @pl.when(step == count - 2)
            def _():
                share[:, lanes[k]] = value

    @pl.loop(0, 4 * chunks)
    def _(event):
        slot, chunk = lax.div(event, chunks), lax.rem(event, chunks)
        for j in range(2):
            @pl.when(slot == 2 + j)
            def _():
                across(j, chunk).wait_recv()
                beside(j, chunk, core).start()

        @pl.when(event == 2 * chunks)
        def _():
            @pl.when(core == 0)
            def _():
                ring_start(early)

        @pl.when(event == 3 * chunks)
        def _():
            @pl.when(core == 0)
            def _():
                ring_start(late)

            @pl.when(core == 1)
            def _():
                ring_start(early)

        for j in range(2):
            @pl.when(slot == 2 + j)
            def _():
                beside(j, chunk, 1 - core).wait_recv()

        rows = pl.ds(pl.multiple_of(event * LANES, LANES), LANES)
        partner_row = 2 * chip + 1 - core
        far_row = 2 * (1 - chip) + slot - 2
        owner = jnp.where(slot == 0, me, jnp.where(slot == 1, partner_row, far_row))
        target = pl.ds(pl.multiple_of((owner * chunks + chunk) * LANES, LANES), LANES)
        mine = pl.ds(pl.multiple_of(me * slab_width, LANES), slab_width)
        slab[:, target] = gram[rows, mine].T
        skipped = jnp.where(core == 0, slot == 3, slot == 1)
        spot = chunk + chunks * jnp.where(core == 0, slot, lax.max(slot - 1, 0))

        @pl.when(jnp.logical_not(skipped))
        def _():
            value = outer_rows(gram[0:block, 0:width], gram[rows, 0:width])
            value = value.astype(jnp.bfloat16)
            for i in range(chunks):
                place_in = spot - i

                @pl.when((place_in >= 0) & (place_in < wide))
                def _():
                    into = pl.ds(pl.multiple_of(place_in * LANES, LANES), LANES)
                    held = slice(i * LANES, (i + 1) * LANES)
                    partial[held, into] = value[held]

        @pl.when(jnp.where(core == 0, slot == 2, slot == 3))
        def _():
            ring_step(chunk, early)

        @pl.when(jnp.where(core == 0, slot == 3, False))
        def _():
            ring_step(chunk, late)

    @pl.when(core == 1)
    def _():
        ring_start(late)

        @pl.loop(0, count - 1)
        def _(step):
            ring_step(step, late)

    def sent():
        for chunk in range(chunks):
            to_partner(chunk).wait_send()
            for j in range(2):
                across(j, chunk).wait_send()
                beside(j, chunk, core).wait_send()
        for step in range(count - 1):
            for k in range(len(lanes)):
                ring_copy(step, k, held_at(running_rows, step, k)).wait_send()

    return sent


def gather_plan(count):
    hops = (count // 2, count - 1 - count // 2)
    ring = [(w, s) for s in range(1, hops[0] + 1) for w in (0, 1) if s <= hops[w]]
    first = [("a",) + hop for hop in ring]
    second = [("b", x) + hop for hop in ring for x in (0, 1)]
    second.sort(key=lambda m: (m[3], m[1], m[2]))
    third = [("ya", 0, 0)] + [("ya",) + hop for hop in ring]
    order = [first[0], first[1], ("start_b",), ("yb",), third[0]]
    order += [first[2], first[3], third[1]]
    rest = first[4:]
    index = 2
    while second or rest:
        for source in (rest, second):
            order += source[:2]
            del source[:2]
        order += third[index : index + 1]
        index += 1
    return hops, order + third[index:]


def gather_names(count):
    _, order = gather_plan(count)
    arrivals = [m for m in order if m[0] != "start_b"]
    partner = [("p",) + m for m in arrivals] + [("p", "own_a"), ("p", "own_b")]
    return {name: number for number, name in enumerate(arrivals + partner)}


def strip_names(bits, u):
    if u == 0:
        near = [[], [("ya", 0, 0), ("yb",)]][bits // 2]
        if bits == 1:
            return [("p", "own_a"), ("p", "own_b")]
    else:
        w, s = (0, -u) if u < 0 else (1, u)
        near = [("ya" if bits & 2 else "a", w, s), ("b", bits // 2, w, s)]
    return [("p",) + m for m in near] if bits & 1 else near


def gather_groups(count, width):
    (long, short), order = gather_plan(count)
    works = []
    for bits in range(4):
        for u in range(-long, short + 1):
            after = u + 1 if u < short else -long
            works.append((bits, u, strip_names(bits, u) + strip_names(bits, after)))
    seen = set()
    groups = []
    for start in range(0, len(order), width):
        events = order[start : start + width]
        due = set(seen)
        seen.update(events)
        ready = []
        for work in list(works):
            names = [m[1:] if m[0] == "p" else m for m in work[2]]
            known = due if work[0] & 1 else seen
            if all(m in known or m[0] in ("own_a", "own_b") for m in names):
                works.remove(work)
                ready.append(work)
        groups.append((events, ready))
    groups.append(([], works))
    return groups


def gather_steps(count, head, strip, land, send_sems, recv_sems):
    me, column = lax.axis_index("row"), lax.axis_index("col")
    place = ring_place(column, count)
    sign = 1 - 2 * lax.rem(me, 2)
    ways = (sign, -sign)
    hops, _ = gather_plan(count)
    names = gather_names(count)

    def where(name, mirrored=False):
        kind = name[0]
        if kind == "p":
            return where(name[1:], True)
        w, s, bits, part = 0, 0, 0, kind[-1]
        if kind in ("a", "ya"):
            w, s = name[1], name[2]
            bits = 2 if kind == "ya" else 0
        elif kind == "b":
            bits, w, s = 2 * name[1], name[2], name[3]
        elif kind == "yb":
            bits = 2
        if mirrored:
            bits = bits + 1
        way = -ways[w] if mirrored else ways[w]
        spot = lax.rem(place - way * s + count, count)
        start = (flipped(me, bits) * count + spot) * strip
        if part == "b":
            return land.at[pl.ds(pl.multiple_of(start + head, 16), strip - head)]
        return land.at[pl.ds(pl.multiple_of(start, 16), head)]

    def target(name):
        if name[0] == "p":
            return {"row": flipped(me, 1)}
        if name[0] in ("ya", "yb"):
            return {"row": flipped(me, 2)}
        w = name[1] if name[0] == "a" else name[2]
        return {"col": ring_column(place + ways[w], count)}

    def copy_of(name, source):
        number = names[name]
        return remote(source, source, send_sems.at[number], recv_sems.at[number], target(name))

    def send(name, held):
        copy_of(name, held).start()

    own_a, own_b = where(("own_a",)), where(("own_b",))

    def begin():
        send(("a", 0, 1), own_a)
        send(("a", 1, 1), own_a)
        send(("yb",), own_b)
        send(("ya", 0, 0), own_a)
        send(("p", "own_a"), own_a)
        send(("p", "own_b"), own_b)

    def arrive(name):
        if name[0] == "start_b":
            send(("b", 0, 0, 1), own_b)
            send(("b", 0, 1, 1), own_b)
            return
        held = where(name)
        copy_of(name, held).wait_recv()
        if name[0] == "a":
            w, s = name[1:]
            if s < hops[w]:
                send(("a", w, s + 1), held)
            send(("ya", w, s), held)
        elif name[0] == "b":
            x, w, s = name[1:]
            if s < hops[w]:
                send(("b", x, w, s + 1), held)
        elif name[0] == "yb":
            send(("b", 1, 0, 1), held)
            send(("b", 1, 1, 1), held)
        send(("p",) + name, held)

    def land_from_partner(name):
        copy_of(name, where(name)).wait_recv()

    def sent():
        for name in names:
            kind = name[1] if name[0] == "p" else name[0]
            copy_of(name, own_a if kind[-1] == "a" else own_b).wait_send()

    return begin, arrive, land_from_partner, sent


def update_kernel(
    count, factor, head, base_ref, out_ref, gram, land, slab_ref, first, rough, exact,
    stage, total, partial, sends, recvs, own_sem, free_sem, out_send, out_recv,
    panel_send, panel_recv, ring_send, ring_recv,
):
    size = gram.shape[0]
    blocks = size // LANES
    strip = size // 4 // count
    wide = land.shape[1] // LANES
    width = slab_ref.shape[0]
    tile = 512 if size % 512 == 0 else LANES
    block = size // 4
    chunks = block // LANES
    me, column = lax.axis_index("row"), lax.axis_index("col")
    place = ring_place(column, count)
    sign = 1 - 2 * lax.rem(me, 2)
    number = me * count + place
    ring = [{"col": ring_column(place + way, count)} for way in (1, -1)]
    near = ring + [{"row": flipped(me, bits)} for bits in (1, 2)]
    meet(pltpu.get_barrier_semaphore(), near + [{"row": flipped(me, 3)}])

    def column_block(index):
        return pl.ds(pl.multiple_of(lax.rem(index, blocks) * LANES, LANES), LANES)

    mine_rows = pl.ds(pl.multiple_of(number * strip, 16), strip)

    def place_block(i, squares):
        here = column_block(i)
        single = double = jnp.zeros((8, LANES), jnp.float32)
        for d in range(wide):
            piece = land[here, d * LANES : (d + 1) * LANES]
            there = column_block(i + d)
            gram[here, there] = piece
            if 0 < d < wide - 1:
                gram[there, here] = piece.T
            if squares:
                value = piece.astype(jnp.float32)
                value = jnp.sum((value * value).reshape(LANES // 8, 8, LANES), axis=0)
                if 0 < d < wide - 1:
                    double = double + value
                else:
                    single = single + value
        if squares:
            total[...] += single + 2.0 * double

    def place_blocks(works, squares):
        if not works:
            return

        @pl.loop(0, len(works))
        def _(step):
            bits, u = works[0][:2]
            code = jnp.int32(bits * 2 * count + u + count)
            for k, (bits, u, _) in enumerate(works[1:], 1):
                code = jnp.where(step == k, bits * 2 * count + u + count, code)
            bits, u = lax.div(code, 2 * count), lax.rem(code, 2 * count) - count
            high, low = lax.div(bits, 2), lax.rem(bits, 2)
            chip, core = lax.div(me, 2), lax.rem(me, 2)
            row = 2 * (chip + high - 2 * chip * high) + (core + low - 2 * core * low)
            way = sign * (1 - 2 * low)
            spot = lax.rem(place + way * u + lax.div(way - 1, 2) + 2 * count, count)

            @pl.when(spot < chunks)
            def _():
                place_block(row * chunks + spot, squares)

    summed_out = sum_share(
        count, wide, base_ref, slab_ref, gram, partial, land.at[mine_rows],
        block + strip * count, panel_send, panel_recv, own_sem, ring_send, ring_recv,
    )
    total[...] = jnp.zeros_like(total)

    def run_groups(groups, steps, squares):
        _, arrive, land_from_partner, sent = steps
        waited = set()
        for events, works in groups:
            for name in events:
                arrive(name)
            for _, _, names in works:
                for name in names:
                    if name[0] == "p" and name not in waited:
                        waited.add(name)
                        land_from_partner(name)
            place_blocks(works, squares)
        sent()

    steps = gather_steps(count, head, strip, land, sends.at[0], recvs.at[0])
    steps[0]()
    summed_out()
    run_groups(gather_groups(count, 4), steps, True)
    for target in near:
        pl.semaphore_signal(
            free_sem, inc=1, device_id=target, device_id_type=pl.DeviceIdType.MESH
        )
    quartic = jnp.sum(jnp.sum(total[...], axis=0, keepdims=True), axis=1, keepdims=True)
    scale = 1.0 / jnp.sqrt(jnp.sqrt(quartic) + EPSILON)
    square = scale * scale

    def times_gram(source, finish, hooks=(), begin=0, tiles=size // tile):
        @pl.loop(0, tiles)
        def _(step):
            for k, calls in enumerate(hooks):
                if calls:
                    @pl.when(step == k)
                    def _():
                        for call in calls:
                            call()

            at = lax.rem(begin + step, size // tile)
            columns = pl.ds(pl.multiple_of(at * tile, tile), tile)
            finish(
                columns,
                jnp.dot(source[...], gram[:, columns], preferred_element_type=jnp.float32),
            )

    part = exact.at[pl.ds(0, strip)]
    left, right = rough.at[pl.ds(0, strip)], first.at[pl.ds(0, strip)]
    mine = gram.at[mine_rows]

    def after_square(columns, value):
        value = value * square * square
        part[:, columns] = (
            COEF_LINEAR * (mine[:, columns].astype(jnp.float32) * square)
            + COEF_CUBIC * value
        )
        left[:, columns] = value.astype(jnp.bfloat16)

    def after_cube(columns, value):
        right[:, columns] = (
            part[:, columns] + COEF_QUINTIC * (value * square)
        ).astype(jnp.bfloat16)

    def after_third(columns, value):
        value = value * square
        part[:, columns] = (
            COEF_LINEAR * right[:, columns].astype(jnp.float32) + COEF_CUBIC * value
        )
        left[:, columns] = value.astype(jnp.bfloat16)

    times_gram(mine, after_square)
    times_gram(left, after_cube)
    times_gram(right, after_third)
    times_gram(
        left,
        after_cube,
        begin=lax.div(number * strip, tile),
        tiles=min(size // tile, pl.cdiv((wide + 1) * LANES, tile) + 1),
    )

    pl.semaphore_wait(free_sem, len(near))
    for group in range(strip // 16):
        sixteenth = number * (strip // 16) + group
        base = lax.div(sixteenth, LANES // 16)
        rows = pl.ds(pl.multiple_of(sixteenth * 16, 16), 16)
        for t in range(wide):
            land[rows, t * LANES : (t + 1) * LANES] = right[
                group * 16 : group * 16 + 16, column_block(base + t)
            ]

    steps = gather_steps(count, head, strip, land, sends.at[1], recvs.at[1])
    steps[0]()
    groups = gather_groups(count, 4)
    slots = size // tile
    paced = [[] for _ in range(2 * slots)]
    early, waiting = [], []
    for k, (events, works) in enumerate(groups):
        if len(early) + len(events) <= 18:
            early += events
            waiting += works
            groups[k] = ([], [])
        else:
            groups[k] = (events, waiting + works)
            break
    for k, name in enumerate(early):
        paced[min(2 * slots - 1, k * 2 * slots // len(early))].append(
            functools.partial(steps[1], name)
        )

    def keep(columns, value):
        value = value * square
        exact[:, columns] = (
            COEF_LINEAR * slab_ref[:, columns].astype(jnp.float32) + COEF_CUBIC * value
        )
        rough[:, columns] = value.astype(jnp.bfloat16)

    def combine(columns, value):
        first[:, columns] = (
            exact[:, columns] + COEF_QUINTIC * (value * square)
        ).astype(jnp.bfloat16)

    times_gram(slab_ref, keep, paced[:slots])
    times_gram(rough, combine, paced[slots:])
    run_groups(groups, steps, False)

    def out_copy(bits, part):
        lanes = pl.ds(pl.multiple_of(me * width + part * LANES, LANES), LANES)
        held = pl.ds(pl.multiple_of(part * LANES, LANES), LANES)
        return remote(
            stage.at[bits, :, held],
            out_ref.at[:, lanes],
            out_send.at[bits - 1, part],
            out_recv.at[bits - 1, part],
            {"row": flipped(me, bits)},
        )

    @pl.loop(0, width // LANES)
    def _(index):
        part = pl.ds(pl.multiple_of(index * LANES, LANES), LANES)

        def after_product(columns, value):
            exact[part, columns] = (
                COEF_LINEAR * first[part, columns].astype(jnp.float32) + COEF_CUBIC * value
            )
            rough[part, columns] = value.astype(jnp.bfloat16)

        times_gram(first.at[part], after_product)

        @pl.loop(0, 4)
        def _(step):
            bits = 3 - step
            chip, core = lax.div(me, 2), lax.rem(me, 2)
            high, low = lax.div(bits, 2), lax.rem(bits, 2)
            owner = 2 * (chip + high - 2 * chip * high) + (core + low - 2 * core * low)
            columns = pl.ds(pl.multiple_of(owner * block, LANES), block)
            value = jnp.dot(
                rough[part, :], gram[:, columns], preferred_element_type=jnp.float32
            )
            value = (exact[part, columns] + COEF_QUINTIC * value) * (scale * factor)
            stage[bits, :, part] = value.astype(jnp.bfloat16).T
            for x in range(1, 4):
                @pl.when(bits == x)
                def _():
                    out_copy(x, index).start()

    lanes = pl.ds(pl.multiple_of(me * width, LANES), width)
    kept = pltpu.make_async_copy(stage.at[0], out_ref.at[:, lanes], own_sem)
    kept.start()
    kept.wait()
    for bits in range(1, 4):
        for part in range(width // LANES):
            out_copy(bits, part).wait()


def updated(base, factor, count, wide):
    block, full_width = base.shape
    size, width = 4 * block, full_width // 4
    strip = block // count
    head = strip * 4 // 7 // 16 * 16
    chunks = block // LANES
    half = pltpu.VMEM((width, size), jnp.bfloat16)
    messages = len(gather_names(count))
    dma = pltpu.SemaphoreType.DMA
    return pl.pallas_call(
        functools.partial(update_kernel, count, factor, head),
        out_shape=jax.ShapeDtypeStruct((block, full_width), jnp.bfloat16),
        in_specs=[pl.BlockSpec(memory_space=pl.ANY)],
        out_specs=pl.BlockSpec(memory_space=pl.ANY),
        scratch_shapes=[
            pltpu.VMEM((size, size), jnp.bfloat16),
            pltpu.VMEM((size, wide * LANES), jnp.bfloat16),
            half,
            half,
            half,
            pltpu.VMEM((width, size), jnp.float32),
            pltpu.VMEM((4, block, width), jnp.bfloat16),
            pltpu.VMEM((8, LANES), jnp.float32),
            pltpu.VMEM((block, wide * LANES), jnp.bfloat16),
            dma((2, messages)),
            dma((2, messages)),
            dma,
            pltpu.SemaphoreType.REGULAR,
            dma((3, width // LANES)),
            dma((3, width // LANES)),
            dma((5, chunks)),
            dma((5, chunks)),
            dma((6, count - 1)),
            dma((6, count - 1)),
        ],
        compiler_params=pltpu.CompilerParams(
            collective_id=1, has_side_effects=True, vmem_limit_bytes=63 * 1024 * 1024
        ),
        name="updated",
    )(base)


def per_device(factor, gradient, momentum):
    rows = lax.axis_size("row")
    grad32 = gradient.astype(jnp.float32)
    buffer = MOMENTUM_DECAY * momentum + grad32
    nesterov = grad32 + MOMENTUM_DECAY * buffer
    base = nesterov.astype(jnp.bfloat16)
    block = base.shape[0]
    count = lax.axis_size("col")
    strip = block // count
    if (
        rows == 4
        and count % 2 == 0
        and count >= 4
        and block % LANES == 0
        and base.shape[1] % (4 * LANES) == 0
        and strip * count == block
        and strip % 16 == 0
        and 32 <= strip < LANES
        and block // LANES + 1 == count
        and base.shape[1] + (2 * block // LANES + 1) * LANES <= 4 * block
    ):
        wide = 4 * block // LANES // 2 + 1
        return (updated(base, factor, count, wide), buffer)
    half = block // 2
    middle = rows // 2
    me = lax.axis_index("row")
    panel = lax.all_gather(base, "row", axis=0, tiled=True)

    def rows_of(offset):
        start = ((me + offset) % rows) * block
        return lax.dynamic_slice_in_dim(panel, start, block, axis=0)

    parts = [outer_rows(base, base)]
    for offset in range(1, middle):
        parts.append(outer_rows(rows_of(offset), base))
    facing = rows_of(middle)
    lower = me < middle
    parts.append(
        outer_rows(
            jnp.where(lower, base[:half], facing[half:]), jnp.where(lower, facing, base)
        )
    )
    partial_value = jnp.concatenate([part.astype(jnp.bfloat16) for part in parts], axis=0)
    count = lax.axis_size("col")
    if block % 128 or count % 2 or count < 4:
        share = lax.psum_scatter(partial_value, "col", scatter_dimension=0, tiled=True)
    else:
        share = ring_sum(partial_value, count)
    shares = lax.all_gather(share, ("row", "col"), axis=0, tiled=True)
    parts = rows
    if block % 128:
        shares = assembled(shares.reshape(rows, -1, block), rows, block)
        parts = 1

    width = panel.shape[1] // rows
    slab = lax.dynamic_slice_in_dim(panel, me * width, width, axis=1)
    update = chain(shares, slab, factor, parts)
    update = lax.all_to_all(update, "row", 0, 1, tiled=True)
    return (update, buffer)


def solution(mesh):
    def whole(gradient, momentum):
        factor = 0.2 * math.sqrt(max(gradient.shape))
        return jax.shard_map(
            functools.partial(per_device, factor),
            mesh=mesh,
            in_specs=(P("row", "col"), P("row", "col")),
            out_specs=(P("row", "col"), P("row", "col")),
            check_vma=False,
        )(gradient, momentum)

    return whole
```

```python
import functools
import math

import jax
import jax.numpy as jnp
from jax import lax
from jax.experimental import pallas as pl
from jax.experimental.pallas import tpu as pltpu
from jax.sharding import PartitionSpec as P

ITERS = 2

MOMENTUM_DECAY = 0.95
EPSILON = 1e-07
COEF_LINEAR = 3.4445
COEF_CUBIC = -4.775
COEF_QUINTIC = 2.0315


def outer_rows(left, right):
    return lax.dot_general(
        left, right, (((1,), (1,)), ((), ())), preferred_element_type=jnp.float32
    )


def direct_blocks(rows, block):
    if rows == 1:
        return [(0, 0, block, 0, 0)]
    half = block // 2
    middle = rows // 2
    found = []
    for j in range(rows):
        for offset in range(middle):
            i = (j + offset) % rows
            found.append((j, offset * block, block, i * block, j * block))
        low, high = min(j, (j + middle) % rows), max(j, (j + middle) % rows)
        top = low * block + (0 if j == low else half)
        found.append((j, middle * block, half, top, high * block))
    return found


def mirrored_blocks(rows):
    if rows == 1:
        return []
    middle = rows // 2
    pairs = [((j + k) % rows, j) for j in range(rows) for k in range(1, middle)]
    return pairs + [(low, low + middle) for low in range(middle)]


def chain_kernel(
    tile, factor, rows, shares_ref, x_ref, out_ref, gram_ref, first, one, two, rough, exact, total, sems
):
    size = gram_ref.shape[0]
    block = size // rows
    stride = shares_ref.shape[0] // rows
    strip = 128
    copies = []
    for number, (owner, start, height, row, column) in enumerate(direct_blocks(rows, block)):
        copies.append(
            pltpu.make_async_copy(
                shares_ref.at[pl.ds(owner * stride + start, height), :],
                gram_ref.at[pl.ds(row, height), pl.ds(column, block)],
                sems.at[number],
            )
        )
    for copy in copies:
        copy.start()
    for copy in copies:
        copy.wait()

    def squares(i, j, mirror):
        def body(step, carry):
            lanes = pl.ds(pl.multiple_of(j * block + step * strip, strip), strip)
            piece = gram_ref[pl.ds(i * block, block), lanes]
            if mirror:
                gram_ref[lanes, pl.ds(i * block, block)] = piece.T
            wide = piece.astype(jnp.float32)
            return carry + jnp.sum(wide * wide, axis=0, keepdims=True)

        return lax.fori_loop(0, block // strip, body, jnp.zeros((1, strip), jnp.float32))

    diagonal = sum(squares(i, i, False) for i in range(rows))
    others = sum(squares(i, j, True) for i, j in mirrored_blocks(rows)) + jnp.zeros_like(diagonal)
    quartic = jnp.sum(diagonal + 2.0 * others, axis=1, keepdims=True)
    scale = 1.0 / jnp.sqrt(jnp.sqrt(quartic) + EPSILON)
    square = scale * scale

    def times_gram(source, finish):
        @pl.loop(0, size // tile)
        def _(step):
            columns = pl.ds(pl.multiple_of(step * tile, tile), tile)
            value = jnp.dot(
                source[...], gram_ref[:, columns], preferred_element_type=jnp.float32
            )
            finish(columns, value * square)

    def polynomial(source, target):
        def keep(columns, value):
            exact[:, columns] = value
            rough[:, columns] = value.astype(jnp.bfloat16)

        def combine(columns, value):
            target[:, columns] = (
                COEF_LINEAR * source[:, columns].astype(jnp.float32)
                + COEF_CUBIC * exact[:, columns]
                + COEF_QUINTIC * value
            ).astype(jnp.bfloat16)

        times_gram(source, keep)
        times_gram(rough, combine)

    width = x_ref.shape[1]
    lanes_step = 128 if width % 128 == 0 else width

    @pl.loop(0, size // strip)
    def _(step):
        chunk = pl.ds(pl.multiple_of(step * strip, strip), strip)
        for lane in range(0, width, lanes_step):
            two[lane : lane + lanes_step, chunk] = x_ref[chunk, lane : lane + lanes_step].T

    polynomial(two, first)
    polynomial(first, one)
    polynomial(one, two)

    def after_product(columns, value):
        total[:, columns] = (
            COEF_LINEAR * first[:, columns].astype(jnp.float32) + COEF_CUBIC * value
        )
        one[:, columns] = value.astype(jnp.bfloat16)

    times_gram(two, after_product)
    polynomial(one, two)
    polynomial(two, one)

    def after_second(columns, value):
        two[:, columns] = (
            (total[:, columns] + COEF_QUINTIC * value) * (scale * factor)
        ).astype(jnp.bfloat16)

    times_gram(one, after_second)

    @pl.loop(0, size // strip)
    def _(step):
        chunk = pl.ds(pl.multiple_of(step * strip, strip), strip)
        for lane in range(0, width, lanes_step):
            out_ref[chunk, lane : lane + lanes_step] = two[lane : lane + lanes_step, chunk].T


def chain(shares, slab, factor, rows):
    size, width = slab.shape
    tile = 512 if size % 512 == 0 else size
    vmem = pl.BlockSpec(memory_space=pltpu.VMEM)
    half = pltpu.VMEM((width, size), jnp.bfloat16)
    full = pltpu.VMEM((width, size), jnp.float32)
    count = rows * (rows // 2 + 1)
    return pl.pallas_call(
        functools.partial(chain_kernel, tile, factor, rows),
        out_shape=jax.ShapeDtypeStruct((size, width), jnp.bfloat16),
        in_specs=[pl.BlockSpec(memory_space=pl.ANY), vmem],
        out_specs=vmem,
        scratch_shapes=[pltpu.VMEM((size, size), jnp.bfloat16)]
        + [half, half, half, half, full, full, pltpu.SemaphoreType.DMA((count,))],
        compiler_params=pltpu.CompilerParams(vmem_limit_bytes=63 * 1024 * 1024),
        name="chain",
    )(shares, slab)


def assembled(shares, rows, block):
    half = block // 2
    middle = rows // 2

    def at(i, j):
        offset = (i - j) % rows
        if offset < middle:
            return shares[j, offset * block : (offset + 1) * block]
        if offset > middle:
            return at(j, i).T
        low, high = min(i, j), max(i, j)
        value = jnp.concatenate([shares[low, -half:], shares[high, -half:]], axis=0)
        return value if i == low else value.T

    return jnp.concatenate(
        [
            jnp.concatenate([at(i, j) for j in range(rows)], axis=1)
            for i in range(rows)
        ],
        axis=0,
    )


def ring_kernel(partial_ref, out_ref, *scratch):
    landed, running, send_sems, recv_sems = scratch[:2], scratch[2:4], scratch[4], scratch[5]
    count = partial_ref.shape[0]
    column = lax.axis_index("col")
    odd, pair = lax.rem(column, 2), lax.div(column, 2)
    place = (1 - odd) * pair + odd * (count - 1 - pair)
    sign = 1 - 2 * lax.rem(lax.axis_index("row"), 2)
    ways = (sign, -sign)
    wide = landed[0].shape[2]
    lanes = (pl.ds(0, wide), pl.ds(wide, landed[1].shape[2]))

    def column_at(spot):
        spot = lax.rem(spot + 2 * count, count)
        back = lax.div(spot, count // 2)
        return (1 - back) * 2 * spot + back * (2 * (count - 1 - spot) + 1)

    barrier = pltpu.get_barrier_semaphore()
    for way in ways:
        pl.semaphore_signal(
            barrier,
            inc=1,
            device_id={"col": column_at(place + way)},
            device_id_type=pl.DeviceIdType.MESH,
        )
    pl.semaphore_wait(barrier, 2)

    def copy_of(step, k, source):
        return pltpu.make_async_remote_copy(
            src_ref=source,
            dst_ref=landed[k].at[step],
            send_sem=send_sems.at[k, step],
            recv_sem=recv_sems.at[k, step],
            device_id={"col": column_at(place + ways[k])},
            device_id_type=pl.DeviceIdType.MESH,
        )

    copies = []
    for k in range(2):
        source = partial_ref.at[column_at(place - ways[k]), :, lanes[k]]
        copies.append([copy_of(0, k, source)])
        copies[k][0].start()
    for step in range(count - 1):
        for k in range(2):
            copies[k][step].wait_recv()
            mine = partial_ref[column_at(place - ways[k] * (step + 2)), :, lanes[k]]
            value = landed[k][step].astype(jnp.float32) + mine.astype(jnp.float32)
            value = value.astype(jnp.bfloat16)
            if step < count - 2:
                running[k][step] = value
                copies[k].append(copy_of(step + 1, k, running[k].at[step]))
                copies[k][step + 1].start()
            else:
                out_ref[:, lanes[k]] = value
    for k in range(2):
        for copy in copies[k]:
            copy.wait_send()


def ring_sum(partial_value, count):
    block = partial_value.shape[1]
    height = partial_value.shape[0] // count
    wide = (block // 128 + 1) // 2 * 128
    vmem = pl.BlockSpec(memory_space=pltpu.VMEM)
    slots = [
        pltpu.VMEM((count - 1, height, width), jnp.bfloat16) for width in (wide, block - wide)
    ]
    sems = pltpu.SemaphoreType.DMA((2, count - 1))
    return pl.pallas_call(
        ring_kernel,
        out_shape=jax.ShapeDtypeStruct((height, block), jnp.bfloat16),
        in_specs=[vmem],
        out_specs=vmem,
        scratch_shapes=slots + slots + [sems, sems],
        compiler_params=pltpu.CompilerParams(
            collective_id=0, has_side_effects=True, vmem_limit_bytes=40 * 1024 * 1024
        ),
        name="ring_sum",
    )(partial_value.reshape(count, height, block))


LANES = 128


def ring_place(column, count):
    odd, pair = lax.rem(column, 2), lax.div(column, 2)
    return (1 - odd) * pair + odd * (count - 1 - pair)


def ring_column(spot, count):
    spot = lax.rem(spot + 2 * count, count)
    back = lax.div(spot, count // 2)
    return (1 - back) * 2 * spot + back * (2 * (count - 1 - spot) + 1)


def flipped(row, bits):
    chip, core = lax.div(row, 2), lax.rem(row, 2)
    if bits & 2:
        chip = 1 - chip
    if bits & 1:
        core = 1 - core
    return 2 * chip + core


def meet(barrier, targets):
    for target in targets:
        pl.semaphore_signal(
            barrier, inc=1, device_id=target, device_id_type=pl.DeviceIdType.MESH
        )
    pl.semaphore_wait(barrier, len(targets))


def remote(source, target, send_sem, recv_sem, device):
    return pltpu.make_async_remote_copy(
        src_ref=source,
        dst_ref=target,
        send_sem=send_sem,
        recv_sem=recv_sem,
        device_id=device,
        device_id_type=pl.DeviceIdType.MESH,
    )


def sum_share(
    count, wide, base_ref, slab, gram, partial, share, running_rows,
    panel_send, panel_recv, own_sem, ring_send, ring_recv,
):
    block, width = base_ref.shape
    chunks = block // LANES
    strip = block // count
    half = LANES // 2
    slab_width = width // 4
    me, column = lax.axis_index("row"), lax.axis_index("col")
    chip, core = lax.div(me, 2), lax.rem(me, 2)
    place = ring_place(column, count)
    sign = 1 - 2 * core
    ways = (sign, -sign)

    def panel(slot, chunk, part=None):
        start = (slot * chunks + chunk) * LANES
        if part is None:
            return gram.at[pl.ds(pl.multiple_of(start, LANES), LANES), pl.ds(0, width)]
        start = pl.multiple_of(start + part * half, half)
        return gram.at[pl.ds(start, half), pl.ds(0, width)]

    def move(kind, chunk, source, target, bits):
        return remote(
            source, target, panel_send.at[kind, chunk], panel_recv.at[kind, chunk],
            {"row": flipped(me, bits)},
        )

    def to_partner(chunk):
        rows = pl.ds(chunk * LANES, LANES)
        return move(0, chunk, base_ref.at[rows], panel(1, chunk), 1)

    def across(j, chunk, own=False):
        source = panel(1, chunk, core)
        if own:
            source = base_ref.at[pl.ds(pl.multiple_of(chunk * LANES + core * half, half), half)]
        return move(1 + j, chunk, source, panel(2 + j, chunk, core), 2)

    def beside(j, chunk, part):
        held = panel(2 + j, chunk, part)
        return move(3 + j, chunk, held, held, 1)

    own = pltpu.make_async_copy(base_ref, gram.at[pl.ds(0, block), pl.ds(0, width)], own_sem)
    own.start()
    for chunk in range(chunks):
        to_partner(chunk).start()

    for k in range(2):
        @pl.when(core == k)
        def _():
            for j in range(2):
                for chunk in range(chunks):
                    if j != k:
                        to_partner(chunk).wait_recv()
                    across(j, chunk, j == k).start()

    own.wait()
    piece = ring_send.shape[0]
    first_half = (chunks + 1) // 2 * 2 * LANES
    starts = [0, first_half // 2]
    rest = wide * LANES - first_half
    step_lanes = pl.cdiv(rest // LANES, 4) * LANES
    starts += list(range(first_half, wide * LANES, step_lanes))
    stops = starts[1:] + [wide * LANES]
    lanes = [pl.ds(start, stop - start) for start, stop in zip(starts, stops)]
    assert len(lanes) <= piece
    early, late = range(2), range(2, len(lanes))

    def strip_at(spot):
        spot = lax.rem(spot + 2 * count, count)
        return pl.ds(pl.multiple_of(spot * strip, 16), strip)

    def held_at(first, step, k):
        rows = pl.ds(pl.multiple_of(first + step * strip, 16), strip)
        return gram.at[rows, pl.ds(width + lanes[k].start, lanes[k].size)]

    def ring_copy(step, k, source):
        return remote(
            source, held_at(block, step, k), ring_send.at[k, step], ring_recv.at[k, step],
            {"col": ring_column(place + ways[k % 2], count)},
        )

    def ring_start(streams):
        for k in streams:
            ring_copy(0, k, partial.at[strip_at(place - ways[k % 2]), lanes[k]]).start()

    def ring_step(step, streams):
        for k in streams:
            landed, running = held_at(block, step, k), held_at(running_rows, step, k)
            ring_copy(step, k, landed).wait_recv()
            mine = partial[strip_at(place - ways[k % 2] * (step + 2)), lanes[k]]
            value = landed[...].astype(jnp.float32) + mine.astype(jnp.float32)
            value = value.astype(jnp.bfloat16)

            @pl.when(step < count - 2)
            def _():
                running[...] = value
                ring_copy(step + 1, k, running).start()

            @pl.when(step == count - 2)
            def _():
                share[:, lanes[k]] = value

    @pl.loop(0, 4 * chunks)
    def _(event):
        slot, chunk = lax.div(event, chunks), lax.rem(event, chunks)
        for j in range(2):
            @pl.when(slot == 2 + j)
            def _():
                across(j, chunk).wait_recv()
                beside(j, chunk, core).start()

        @pl.when(event == 2 * chunks)
        def _():
            @pl.when(core == 0)
            def _():
                ring_start(early)

        @pl.when(event == 3 * chunks)
        def _():
            @pl.when(core == 0)
            def _():
                ring_start(late)

            @pl.when(core == 1)
            def _():
                ring_start(early)

        for j in range(2):
            @pl.when(slot == 2 + j)
            def _():
                beside(j, chunk, 1 - core).wait_recv()

        rows = pl.ds(pl.multiple_of(event * LANES, LANES), LANES)
        partner_row = 2 * chip + 1 - core
        far_row = 2 * (1 - chip) + slot - 2
        owner = jnp.where(slot == 0, me, jnp.where(slot == 1, partner_row, far_row))
        target = pl.ds(pl.multiple_of((owner * chunks + chunk) * LANES, LANES), LANES)
        mine = pl.ds(pl.multiple_of(me * slab_width, LANES), slab_width)
        slab[:, target] = gram[rows, mine].T
        skipped = jnp.where(core == 0, slot == 3, slot == 1)
        spot = chunk + chunks * jnp.where(core == 0, slot, lax.max(slot - 1, 0))

        @pl.when(jnp.logical_not(skipped))
        def _():
            value = outer_rows(gram[0:block, 0:width], gram[rows, 0:width])
            value = value.astype(jnp.bfloat16)
            for i in range(chunks):
                place_in = spot - i

                @pl.when((place_in >= 0) & (place_in < wide))
                def _():
                    into = pl.ds(pl.multiple_of(place_in * LANES, LANES), LANES)
                    held = slice(i * LANES, (i + 1) * LANES)
                    partial[held, into] = value[held]

        @pl.when(jnp.where(core == 0, slot == 2, slot == 3))
        def _():
            ring_step(chunk, early)

        @pl.when(jnp.where(core == 0, slot == 3, False))
        def _():
            ring_step(chunk, late)

    @pl.when(core == 1)
    def _():
        ring_start(late)

        @pl.loop(0, count - 1)
        def _(step):
            ring_step(step, late)

    def sent():
        for chunk in range(chunks):
            to_partner(chunk).wait_send()
            for j in range(2):
                across(j, chunk).wait_send()
                beside(j, chunk, core).wait_send()
        for step in range(count - 1):
            for k in range(len(lanes)):
                ring_copy(step, k, held_at(running_rows, step, k)).wait_send()

    return sent


def gather_plan(count):
    hops = (count // 2, count - 1 - count // 2)
    ring = [(w, s) for s in range(1, hops[0] + 1) for w in (0, 1) if s <= hops[w]]
    first = [("a",) + hop for hop in ring]
    second = [("b", x) + hop for hop in ring for x in (0, 1)]
    second.sort(key=lambda m: (m[3], m[1], m[2]))
    third = [("ya", 0, 0)] + [("ya",) + hop for hop in ring]
    order = [first[0], first[1], ("start_b",), ("yb",), third[0]]
    order += [first[2], first[3], third[1]]
    rest = first[4:]
    index = 2
    while second or rest:
        for source in (rest, second):
            order += source[:2]
            del source[:2]
        order += third[index : index + 1]
        index += 1
    return hops, order + third[index:]


def gather_names(count):
    _, order = gather_plan(count)
    arrivals = [m for m in order if m[0] != "start_b"]
    partner = [("p",) + m for m in arrivals] + [("p", "own_a"), ("p", "own_b")]
    return {name: number for number, name in enumerate(arrivals + partner)}


def strip_names(bits, u):
    if u == 0:
        near = [[], [("ya", 0, 0), ("yb",)]][bits // 2]
        if bits == 1:
            return [("p", "own_a"), ("p", "own_b")]
    else:
        w, s = (0, -u) if u < 0 else (1, u)
        near = [("ya" if bits & 2 else "a", w, s), ("b", bits // 2, w, s)]
    return [("p",) + m for m in near] if bits & 1 else near


def gather_groups(count, width):
    (long, short), order = gather_plan(count)
    works = []
    for bits in range(4):
        for u in range(-long, short + 1):
            after = u + 1 if u < short else -long
            works.append((bits, u, strip_names(bits, u) + strip_names(bits, after)))
    seen = set()
    groups = []
    for start in range(0, len(order), width):
        events = order[start : start + width]
        due = set(seen)
        seen.update(events)
        ready = []
        for work in list(works):
            names = [m[1:] if m[0] == "p" else m for m in work[2]]
            known = due if work[0] & 1 else seen
            if all(m in known or m[0] in ("own_a", "own_b") for m in names):
                works.remove(work)
                ready.append(work)
        groups.append((events, ready))
    groups.append(([], works))
    return groups


def gather_steps(count, head, strip, land, send_sems, recv_sems):
    me, column = lax.axis_index("row"), lax.axis_index("col")
    place = ring_place(column, count)
    sign = 1 - 2 * lax.rem(me, 2)
    ways = (sign, -sign)
    hops, _ = gather_plan(count)
    names = gather_names(count)

    def where(name, mirrored=False):
        kind = name[0]
        if kind == "p":
            return where(name[1:], True)
        w, s, bits, part = 0, 0, 0, kind[-1]
        if kind in ("a", "ya"):
            w, s = name[1], name[2]
            bits = 2 if kind == "ya" else 0
        elif kind == "b":
            bits, w, s = 2 * name[1], name[2], name[3]
        elif kind == "yb":
            bits = 2
        if mirrored:
            bits = bits + 1
        way = -ways[w] if mirrored else ways[w]
        spot = lax.rem(place - way * s + count, count)
        start = (flipped(me, bits) * count + spot) * strip
        if part == "b":
            return land.at[pl.ds(pl.multiple_of(start + head, 16), strip - head)]
        return land.at[pl.ds(pl.multiple_of(start, 16), head)]

    def target(name):
        if name[0] == "p":
            return {"row": flipped(me, 1)}
        if name[0] in ("ya", "yb"):
            return {"row": flipped(me, 2)}
        w = name[1] if name[0] == "a" else name[2]
        return {"col": ring_column(place + ways[w], count)}

    def copy_of(name, source):
        number = names[name]
        return remote(source, source, send_sems.at[number], recv_sems.at[number], target(name))

    def send(name, held):
        copy_of(name, held).start()

    own_a, own_b = where(("own_a",)), where(("own_b",))

    def begin():
        send(("a", 0, 1), own_a)
        send(("a", 1, 1), own_a)
        send(("yb",), own_b)
        send(("ya", 0, 0), own_a)
        send(("p", "own_a"), own_a)
        send(("p", "own_b"), own_b)

    def arrive(name):
        if name[0] == "start_b":
            send(("b", 0, 0, 1), own_b)
            send(("b", 0, 1, 1), own_b)
            return
        held = where(name)
        copy_of(name, held).wait_recv()
        if name[0] == "a":
            w, s = name[1:]
            if s < hops[w]:
                send(("a", w, s + 1), held)
            send(("ya", w, s), held)
        elif name[0] == "b":
            x, w, s = name[1:]
            if s < hops[w]:
                send(("b", x, w, s + 1), held)
        elif name[0] == "yb":
            send(("b", 1, 0, 1), held)
            send(("b", 1, 1, 1), held)
        send(("p",) + name, held)

    def land_from_partner(name):
        copy_of(name, where(name)).wait_recv()

    def sent():
        for name in names:
            kind = name[1] if name[0] == "p" else name[0]
            copy_of(name, own_a if kind[-1] == "a" else own_b).wait_send()

    return begin, arrive, land_from_partner, sent


def update_kernel(
    count, factor, head, base_ref, out_ref, gram, land, slab_ref, first, rough, exact,
    stage, total, partial, sends, recvs, own_sem, free_sem, out_send, out_recv,
    panel_send, panel_recv, ring_send, ring_recv,
):
    size = gram.shape[0]
    blocks = size // LANES
    strip = size // 4 // count
    wide = land.shape[1] // LANES
    width = slab_ref.shape[0]
    tile = 512 if size % 512 == 0 else LANES
    block = size // 4
    chunks = block // LANES
    me, column = lax.axis_index("row"), lax.axis_index("col")
    place = ring_place(column, count)
    sign = 1 - 2 * lax.rem(me, 2)
    number = me * count + place
    ring = [{"col": ring_column(place + way, count)} for way in (1, -1)]
    near = ring + [{"row": flipped(me, bits)} for bits in (1, 2)]
    meet(pltpu.get_barrier_semaphore(), near + [{"row": flipped(me, 3)}])

    def column_block(index):
        return pl.ds(pl.multiple_of(lax.rem(index, blocks) * LANES, LANES), LANES)

    mine_rows = pl.ds(pl.multiple_of(number * strip, 16), strip)

    def place_block(i, squares):
        here = column_block(i)
        single = double = jnp.zeros((8, LANES), jnp.float32)
        for d in range(wide):
            piece = land[here, d * LANES : (d + 1) * LANES]
            there = column_block(i + d)
            gram[here, there] = piece
            if 0 < d < wide - 1:
                gram[there, here] = piece.T
            if squares:
                value = piece.astype(jnp.float32)
                value = jnp.sum((value * value).reshape(LANES // 8, 8, LANES), axis=0)
                if 0 < d < wide - 1:
                    double = double + value
                else:
                    single = single + value
        if squares:
            total[...] += single + 2.0 * double

    def place_blocks(works, squares):
        if not works:
            return

        @pl.loop(0, len(works))
        def _(step):
            bits, u = works[0][:2]
            code = jnp.int32(bits * 2 * count + u + count)
            for k, (bits, u, _) in enumerate(works[1:], 1):
                code = jnp.where(step == k, bits * 2 * count + u + count, code)
            bits, u = lax.div(code, 2 * count), lax.rem(code, 2 * count) - count
            high, low = lax.div(bits, 2), lax.rem(bits, 2)
            chip, core = lax.div(me, 2), lax.rem(me, 2)
            row = 2 * (chip + high - 2 * chip * high) + (core + low - 2 * core * low)
            way = sign * (1 - 2 * low)
            spot = lax.rem(place + way * u + lax.div(way - 1, 2) + 2 * count, count)

            @pl.when(spot < chunks)
            def _():
                place_block(row * chunks + spot, squares)

    summed_out = sum_share(
        count, wide, base_ref, slab_ref, gram, partial, land.at[mine_rows],
        block + strip * count, panel_send, panel_recv, own_sem, ring_send, ring_recv,
    )
    total[...] = jnp.zeros_like(total)

    def run_groups(groups, steps, squares):
        _, arrive, land_from_partner, sent = steps
        waited = set()
        for events, works in groups:
            for name in events:
                arrive(name)
            for _, _, names in works:
                for name in names:
                    if name[0] == "p" and name not in waited:
                        waited.add(name)
                        land_from_partner(name)
            place_blocks(works, squares)
        sent()

    steps = gather_steps(count, head, strip, land, sends.at[0], recvs.at[0])
    steps[0]()
    summed_out()
    run_groups(gather_groups(count, 4), steps, True)
    for target in near:
        pl.semaphore_signal(
            free_sem, inc=1, device_id=target, device_id_type=pl.DeviceIdType.MESH
        )
    quartic = jnp.sum(jnp.sum(total[...], axis=0, keepdims=True), axis=1, keepdims=True)
    scale = 1.0 / jnp.sqrt(jnp.sqrt(quartic) + EPSILON)
    square = scale * scale

    def times_gram(source, finish, hooks=(), begin=0, tiles=size // tile):
        @pl.loop(0, tiles)
        def _(step):
            for k, calls in enumerate(hooks):
                if calls:
                    @pl.when(step == k)
                    def _():
                        for call in calls:
                            call()

            at = lax.rem(begin + step, size // tile)
            columns = pl.ds(pl.multiple_of(at * tile, tile), tile)
            finish(
                columns,
                jnp.dot(source[...], gram[:, columns], preferred_element_type=jnp.float32),
            )

    part = exact.at[pl.ds(0, strip)]
    left, right = rough.at[pl.ds(0, strip)], first.at[pl.ds(0, strip)]
    mine = gram.at[mine_rows]

    def after_square(columns, value):
        value = value * square * square
        part[:, columns] = (
            COEF_LINEAR * (mine[:, columns].astype(jnp.float32) * square)
            + COEF_CUBIC * value
        )
        left[:, columns] = value.astype(jnp.bfloat16)

    def after_cube(columns, value):
        right[:, columns] = (
            part[:, columns] + COEF_QUINTIC * (value * square)
        ).astype(jnp.bfloat16)

    def after_third(columns, value):
        value = value * square
        part[:, columns] = (
            COEF_LINEAR * right[:, columns].astype(jnp.float32) + COEF_CUBIC * value
        )
        left[:, columns] = value.astype(jnp.bfloat16)

    times_gram(mine, after_square)
    times_gram(left, after_cube)
    times_gram(right, after_third)
    times_gram(
        left,
        after_cube,
        begin=lax.div(number * strip, tile),
        tiles=min(size // tile, pl.cdiv((wide + 1) * LANES, tile) + 1),
    )

    pl.semaphore_wait(free_sem, len(near))
    for group in range(strip // 16):
        sixteenth = number * (strip // 16) + group
        base = lax.div(sixteenth, LANES // 16)
        rows = pl.ds(pl.multiple_of(sixteenth * 16, 16), 16)
        for t in range(wide):
            land[rows, t * LANES : (t + 1) * LANES] = right[
                group * 16 : group * 16 + 16, column_block(base + t)
            ]

    steps = gather_steps(count, head, strip, land, sends.at[1], recvs.at[1])
    steps[0]()
    groups = gather_groups(count, 4)
    slots = size // tile
    paced = [[] for _ in range(2 * slots)]
    early, waiting = [], []
    for k, (events, works) in enumerate(groups):
        if len(early) + len(events) <= 20:
            early += events
            waiting += works
            groups[k] = ([], [])
        else:
            groups[k] = (events, waiting + works)
            break
    for k, name in enumerate(early):
        paced[slots // 2 + k * (2 * slots - slots // 2) // len(early)].append(
            functools.partial(steps[1], name)
        )

    def keep(columns, value):
        value = value * square
        exact[:, columns] = (
            COEF_LINEAR * slab_ref[:, columns].astype(jnp.float32) + COEF_CUBIC * value
        )
        rough[:, columns] = value.astype(jnp.bfloat16)

    def combine(columns, value):
        first[:, columns] = (
            exact[:, columns] + COEF_QUINTIC * (value * square)
        ).astype(jnp.bfloat16)

    times_gram(slab_ref, keep, paced[:slots])
    times_gram(rough, combine, paced[slots:])
    run_groups(groups, steps, False)

    def out_copy(bits, part):
        lanes = pl.ds(pl.multiple_of(me * width + part * LANES, LANES), LANES)
        held = pl.ds(pl.multiple_of(part * LANES, LANES), LANES)
        return remote(
            stage.at[bits, :, held],
            out_ref.at[:, lanes],
            out_send.at[bits - 1, part],
            out_recv.at[bits - 1, part],
            {"row": flipped(me, bits)},
        )

    @pl.loop(0, width // LANES)
    def _(index):
        part = pl.ds(pl.multiple_of(index * LANES, LANES), LANES)

        def after_product(columns, value):
            exact[part, columns] = (
                COEF_LINEAR * first[part, columns].astype(jnp.float32) + COEF_CUBIC * value
            )
            rough[part, columns] = value.astype(jnp.bfloat16)

        times_gram(first.at[part], after_product)

        @pl.loop(0, 4)
        def _(step):
            bits = 3 - step
            chip, core = lax.div(me, 2), lax.rem(me, 2)
            high, low = lax.div(bits, 2), lax.rem(bits, 2)
            owner = 2 * (chip + high - 2 * chip * high) + (core + low - 2 * core * low)
            columns = pl.ds(pl.multiple_of(owner * block, LANES), block)
            value = jnp.dot(
                rough[part, :], gram[:, columns], preferred_element_type=jnp.float32
            )
            value = (exact[part, columns] + COEF_QUINTIC * value) * (scale * factor)
            stage[bits, :, part] = value.astype(jnp.bfloat16).T
            for x in range(1, 4):
                @pl.when(bits == x)
                def _():
                    out_copy(x, index).start()

    lanes = pl.ds(pl.multiple_of(me * width, LANES), width)
    kept = pltpu.make_async_copy(stage.at[0], out_ref.at[:, lanes], own_sem)
    kept.start()
    kept.wait()
    for bits in range(1, 4):
        for part in range(width // LANES):
            out_copy(bits, part).wait()


def updated(base, factor, count, wide):
    block, full_width = base.shape
    size, width = 4 * block, full_width // 4
    strip = block // count
    head = strip * 4 // 7 // 16 * 16
    chunks = block // LANES
    half = pltpu.VMEM((width, size), jnp.bfloat16)
    messages = len(gather_names(count))
    dma = pltpu.SemaphoreType.DMA
    return pl.pallas_call(
        functools.partial(update_kernel, count, factor, head),
        out_shape=jax.ShapeDtypeStruct((block, full_width), jnp.bfloat16),
        in_specs=[pl.BlockSpec(memory_space=pl.ANY)],
        out_specs=pl.BlockSpec(memory_space=pl.ANY),
        scratch_shapes=[
            pltpu.VMEM((size, size), jnp.bfloat16),
            pltpu.VMEM((size, wide * LANES), jnp.bfloat16),
            half,
            half,
            half,
            pltpu.VMEM((width, size), jnp.float32),
            pltpu.VMEM((4, block, width), jnp.bfloat16),
            pltpu.VMEM((8, LANES), jnp.float32),
            pltpu.VMEM((block, wide * LANES), jnp.bfloat16),
            dma((2, messages)),
            dma((2, messages)),
            dma,
            pltpu.SemaphoreType.REGULAR,
            dma((3, width // LANES)),
            dma((3, width // LANES)),
            dma((5, chunks)),
            dma((5, chunks)),
            dma((6, count - 1)),
            dma((6, count - 1)),
        ],
        compiler_params=pltpu.CompilerParams(
            collective_id=1, has_side_effects=True, vmem_limit_bytes=63 * 1024 * 1024
        ),
        name="updated",
    )(base)


def per_device(factor, gradient, momentum):
    rows = lax.axis_size("row")
    grad32 = gradient.astype(jnp.float32)
    buffer = MOMENTUM_DECAY * momentum + grad32
    nesterov = grad32 + MOMENTUM_DECAY * buffer
    base = nesterov.astype(jnp.bfloat16)
    block = base.shape[0]
    count = lax.axis_size("col")
    strip = block // count
    if (
        rows == 4
        and count % 2 == 0
        and count >= 4
        and block % LANES == 0
        and base.shape[1] % (4 * LANES) == 0
        and strip * count == block
        and strip % 16 == 0
        and 32 <= strip < LANES
        and block // LANES + 1 == count
        and base.shape[1] + (2 * block // LANES + 1) * LANES <= 4 * block
    ):
        wide = 4 * block // LANES // 2 + 1
        return (updated(base, factor, count, wide), buffer)
    half = block // 2
    middle = rows // 2
    me = lax.axis_index("row")
    panel = lax.all_gather(base, "row", axis=0, tiled=True)

    def rows_of(offset):
        start = ((me + offset) % rows) * block
        return lax.dynamic_slice_in_dim(panel, start, block, axis=0)

    parts = [outer_rows(base, base)]
    for offset in range(1, middle):
        parts.append(outer_rows(rows_of(offset), base))
    facing = rows_of(middle)
    lower = me < middle
    parts.append(
        outer_rows(
            jnp.where(lower, base[:half], facing[half:]), jnp.where(lower, facing, base)
        )
    )
    partial_value = jnp.concatenate([part.astype(jnp.bfloat16) for part in parts], axis=0)
    count = lax.axis_size("col")
    if block % 128 or count % 2 or count < 4:
        share = lax.psum_scatter(partial_value, "col", scatter_dimension=0, tiled=True)
    else:
        share = ring_sum(partial_value, count)
    shares = lax.all_gather(share, ("row", "col"), axis=0, tiled=True)
    parts = rows
    if block % 128:
        shares = assembled(shares.reshape(rows, -1, block), rows, block)
        parts = 1

    width = panel.shape[1] // rows
    slab = lax.dynamic_slice_in_dim(panel, me * width, width, axis=1)
    update = chain(shares, slab, factor, parts)
    update = lax.all_to_all(update, "row", 0, 1, tiled=True)
    return (update, buffer)


def solution(mesh):
    def whole(gradient, momentum):
        factor = 0.2 * math.sqrt(max(gradient.shape))
        return jax.shard_map(
            functools.partial(per_device, factor),
            mesh=mesh,
            in_specs=(P("row", "col"), P("row", "col")),
            out_specs=(P("row", "col"), P("row", "col")),
            check_vma=False,
        )(gradient, momentum)

    return whole
```

```python
import functools
import math

import jax
import jax.numpy as jnp
from jax import lax
from jax.experimental import pallas as pl
from jax.experimental.pallas import tpu as pltpu
from jax.sharding import PartitionSpec as P

ITERS = 2

MOMENTUM_DECAY = 0.95
EPSILON = 1e-07
COEF_LINEAR = 3.4445
COEF_CUBIC = -4.775
COEF_QUINTIC = 2.0315


def outer_rows(left, right):
    return lax.dot_general(
        left, right, (((1,), (1,)), ((), ())), preferred_element_type=jnp.float32
    )


def direct_blocks(rows, block):
    if rows == 1:
        return [(0, 0, block, 0, 0)]
    half = block // 2
    middle = rows // 2
    found = []
    for j in range(rows):
        for offset in range(middle):
            i = (j + offset) % rows
            found.append((j, offset * block, block, i * block, j * block))
        low, high = min(j, (j + middle) % rows), max(j, (j + middle) % rows)
        top = low * block + (0 if j == low else half)
        found.append((j, middle * block, half, top, high * block))
    return found


def mirrored_blocks(rows):
    if rows == 1:
        return []
    middle = rows // 2
    pairs = [((j + k) % rows, j) for j in range(rows) for k in range(1, middle)]
    return pairs + [(low, low + middle) for low in range(middle)]


def chain_kernel(
    tile, factor, rows, shares_ref, x_ref, out_ref, gram_ref, first, one, two, rough, exact, total, sems
):
    size = gram_ref.shape[0]
    block = size // rows
    stride = shares_ref.shape[0] // rows
    strip = 128
    copies = []
    for number, (owner, start, height, row, column) in enumerate(direct_blocks(rows, block)):
        copies.append(
            pltpu.make_async_copy(
                shares_ref.at[pl.ds(owner * stride + start, height), :],
                gram_ref.at[pl.ds(row, height), pl.ds(column, block)],
                sems.at[number],
            )
        )
    for copy in copies:
        copy.start()
    for copy in copies:
        copy.wait()

    def squares(i, j, mirror):
        def body(step, carry):
            lanes = pl.ds(pl.multiple_of(j * block + step * strip, strip), strip)
            piece = gram_ref[pl.ds(i * block, block), lanes]
            if mirror:
                gram_ref[lanes, pl.ds(i * block, block)] = piece.T
            wide = piece.astype(jnp.float32)
            return carry + jnp.sum(wide * wide, axis=0, keepdims=True)

        return lax.fori_loop(0, block // strip, body, jnp.zeros((1, strip), jnp.float32))

    diagonal = sum(squares(i, i, False) for i in range(rows))
    others = sum(squares(i, j, True) for i, j in mirrored_blocks(rows)) + jnp.zeros_like(diagonal)
    quartic = jnp.sum(diagonal + 2.0 * others, axis=1, keepdims=True)
    scale = 1.0 / jnp.sqrt(jnp.sqrt(quartic) + EPSILON)
    square = scale * scale

    def times_gram(source, finish):
        @pl.loop(0, size // tile)
        def _(step):
            columns = pl.ds(pl.multiple_of(step * tile, tile), tile)
            value = jnp.dot(
                source[...], gram_ref[:, columns], preferred_element_type=jnp.float32
            )
            finish(columns, value * square)

    def polynomial(source, target):
        def keep(columns, value):
            exact[:, columns] = value
            rough[:, columns] = value.astype(jnp.bfloat16)

        def combine(columns, value):
            target[:, columns] = (
                COEF_LINEAR * source[:, columns].astype(jnp.float32)
                + COEF_CUBIC * exact[:, columns]
                + COEF_QUINTIC * value
            ).astype(jnp.bfloat16)

        times_gram(source, keep)
        times_gram(rough, combine)

    width = x_ref.shape[1]
    lanes_step = 128 if width % 128 == 0 else width

    @pl.loop(0, size // strip)
    def _(step):
        chunk = pl.ds(pl.multiple_of(step * strip, strip), strip)
        for lane in range(0, width, lanes_step):
            two[lane : lane + lanes_step, chunk] = x_ref[chunk, lane : lane + lanes_step].T

    polynomial(two, first)
    polynomial(first, one)
    polynomial(one, two)

    def after_product(columns, value):
        total[:, columns] = (
            COEF_LINEAR * first[:, columns].astype(jnp.float32) + COEF_CUBIC * value
        )
        one[:, columns] = value.astype(jnp.bfloat16)

    times_gram(two, after_product)
    polynomial(one, two)
    polynomial(two, one)

    def after_second(columns, value):
        two[:, columns] = (
            (total[:, columns] + COEF_QUINTIC * value) * (scale * factor)
        ).astype(jnp.bfloat16)

    times_gram(one, after_second)

    @pl.loop(0, size // strip)
    def _(step):
        chunk = pl.ds(pl.multiple_of(step * strip, strip), strip)
        for lane in range(0, width, lanes_step):
            out_ref[chunk, lane : lane + lanes_step] = two[lane : lane + lanes_step, chunk].T


def chain(shares, slab, factor, rows):
    size, width = slab.shape
    tile = 512 if size % 512 == 0 else size
    vmem = pl.BlockSpec(memory_space=pltpu.VMEM)
    half = pltpu.VMEM((width, size), jnp.bfloat16)
    full = pltpu.VMEM((width, size), jnp.float32)
    count = rows * (rows // 2 + 1)
    return pl.pallas_call(
        functools.partial(chain_kernel, tile, factor, rows),
        out_shape=jax.ShapeDtypeStruct((size, width), jnp.bfloat16),
        in_specs=[pl.BlockSpec(memory_space=pl.ANY), vmem],
        out_specs=vmem,
        scratch_shapes=[pltpu.VMEM((size, size), jnp.bfloat16)]
        + [half, half, half, half, full, full, pltpu.SemaphoreType.DMA((count,))],
        compiler_params=pltpu.CompilerParams(vmem_limit_bytes=63 * 1024 * 1024),
        name="chain",
    )(shares, slab)


def assembled(shares, rows, block):
    half = block // 2
    middle = rows // 2

    def at(i, j):
        offset = (i - j) % rows
        if offset < middle:
            return shares[j, offset * block : (offset + 1) * block]
        if offset > middle:
            return at(j, i).T
        low, high = min(i, j), max(i, j)
        value = jnp.concatenate([shares[low, -half:], shares[high, -half:]], axis=0)
        return value if i == low else value.T

    return jnp.concatenate(
        [
            jnp.concatenate([at(i, j) for j in range(rows)], axis=1)
            for i in range(rows)
        ],
        axis=0,
    )


def ring_kernel(partial_ref, out_ref, *scratch):
    landed, running, send_sems, recv_sems = scratch[:2], scratch[2:4], scratch[4], scratch[5]
    count = partial_ref.shape[0]
    column = lax.axis_index("col")
    odd, pair = lax.rem(column, 2), lax.div(column, 2)
    place = (1 - odd) * pair + odd * (count - 1 - pair)
    sign = 1 - 2 * lax.rem(lax.axis_index("row"), 2)
    ways = (sign, -sign)
    wide = landed[0].shape[2]
    lanes = (pl.ds(0, wide), pl.ds(wide, landed[1].shape[2]))

    def column_at(spot):
        spot = lax.rem(spot + 2 * count, count)
        back = lax.div(spot, count // 2)
        return (1 - back) * 2 * spot + back * (2 * (count - 1 - spot) + 1)

    barrier = pltpu.get_barrier_semaphore()
    for way in ways:
        pl.semaphore_signal(
            barrier,
            inc=1,
            device_id={"col": column_at(place + way)},
            device_id_type=pl.DeviceIdType.MESH,
        )
    pl.semaphore_wait(barrier, 2)

    def copy_of(step, k, source):
        return pltpu.make_async_remote_copy(
            src_ref=source,
            dst_ref=landed[k].at[step],
            send_sem=send_sems.at[k, step],
            recv_sem=recv_sems.at[k, step],
            device_id={"col": column_at(place + ways[k])},
            device_id_type=pl.DeviceIdType.MESH,
        )

    copies = []
    for k in range(2):
        source = partial_ref.at[column_at(place - ways[k]), :, lanes[k]]
        copies.append([copy_of(0, k, source)])
        copies[k][0].start()
    for step in range(count - 1):
        for k in range(2):
            copies[k][step].wait_recv()
            mine = partial_ref[column_at(place - ways[k] * (step + 2)), :, lanes[k]]
            value = landed[k][step].astype(jnp.float32) + mine.astype(jnp.float32)
            value = value.astype(jnp.bfloat16)
            if step < count - 2:
                running[k][step] = value
                copies[k].append(copy_of(step + 1, k, running[k].at[step]))
                copies[k][step + 1].start()
            else:
                out_ref[:, lanes[k]] = value
    for k in range(2):
        for copy in copies[k]:
            copy.wait_send()


def ring_sum(partial_value, count):
    block = partial_value.shape[1]
    height = partial_value.shape[0] // count
    wide = (block // 128 + 1) // 2 * 128
    vmem = pl.BlockSpec(memory_space=pltpu.VMEM)
    slots = [
        pltpu.VMEM((count - 1, height, width), jnp.bfloat16) for width in (wide, block - wide)
    ]
    sems = pltpu.SemaphoreType.DMA((2, count - 1))
    return pl.pallas_call(
        ring_kernel,
        out_shape=jax.ShapeDtypeStruct((height, block), jnp.bfloat16),
        in_specs=[vmem],
        out_specs=vmem,
        scratch_shapes=slots + slots + [sems, sems],
        compiler_params=pltpu.CompilerParams(
            collective_id=0, has_side_effects=True, vmem_limit_bytes=40 * 1024 * 1024
        ),
        name="ring_sum",
    )(partial_value.reshape(count, height, block))


LANES = 128


def ring_place(column, count):
    odd, pair = lax.rem(column, 2), lax.div(column, 2)
    return (1 - odd) * pair + odd * (count - 1 - pair)


def ring_column(spot, count):
    spot = lax.rem(spot + 2 * count, count)
    back = lax.div(spot, count // 2)
    return (1 - back) * 2 * spot + back * (2 * (count - 1 - spot) + 1)


def flipped(row, bits):
    chip, core = lax.div(row, 2), lax.rem(row, 2)
    if bits & 2:
        chip = 1 - chip
    if bits & 1:
        core = 1 - core
    return 2 * chip + core


def meet(barrier, targets):
    for target in targets:
        pl.semaphore_signal(
            barrier, inc=1, device_id=target, device_id_type=pl.DeviceIdType.MESH
        )
    pl.semaphore_wait(barrier, len(targets))


def remote(source, target, send_sem, recv_sem, device):
    return pltpu.make_async_remote_copy(
        src_ref=source,
        dst_ref=target,
        send_sem=send_sem,
        recv_sem=recv_sem,
        device_id=device,
        device_id_type=pl.DeviceIdType.MESH,
    )


def sum_share(
    count, wide, base_ref, slab, gram, partial, share, running_rows,
    panel_send, panel_recv, own_sem, ring_send, ring_recv,
):
    block, width = base_ref.shape
    chunks = block // LANES
    strip = block // count
    half = LANES // 2
    slab_width = width // 4
    me, column = lax.axis_index("row"), lax.axis_index("col")
    chip, core = lax.div(me, 2), lax.rem(me, 2)
    place = ring_place(column, count)
    sign = 1 - 2 * core
    ways = (sign, -sign)

    def panel(slot, chunk, part=None):
        start = (slot * chunks + chunk) * LANES
        if part is None:
            return gram.at[pl.ds(pl.multiple_of(start, LANES), LANES), pl.ds(0, width)]
        start = pl.multiple_of(start + part * half, half)
        return gram.at[pl.ds(start, half), pl.ds(0, width)]

    def move(kind, chunk, source, target, bits):
        return remote(
            source, target, panel_send.at[kind, chunk], panel_recv.at[kind, chunk],
            {"row": flipped(me, bits)},
        )

    def to_partner(chunk):
        rows = pl.ds(chunk * LANES, LANES)
        return move(0, chunk, base_ref.at[rows], panel(1, chunk), 1)

    def across(j, chunk, own=False):
        source = panel(1, chunk, core)
        if own:
            source = base_ref.at[pl.ds(pl.multiple_of(chunk * LANES + core * half, half), half)]
        return move(1 + j, chunk, source, panel(2 + j, chunk, core), 2)

    def beside(j, chunk, part):
        held = panel(2 + j, chunk, part)
        return move(3 + j, chunk, held, held, 1)

    own = pltpu.make_async_copy(base_ref, gram.at[pl.ds(0, block), pl.ds(0, width)], own_sem)
    own.start()
    for chunk in range(chunks):
        to_partner(chunk).start()

    for k in range(2):
        @pl.when(core == k)
        def _():
            for j in range(2):
                for chunk in range(chunks):
                    if j != k:
                        to_partner(chunk).wait_recv()
                    across(j, chunk, j == k).start()

    own.wait()
    piece = ring_send.shape[0]
    first_half = (chunks + 1) // 2 * 2 * LANES
    starts = [0, first_half // 2]
    rest = wide * LANES - first_half
    step_lanes = pl.cdiv(rest // LANES, 4) * LANES
    starts += list(range(first_half, wide * LANES, step_lanes))
    stops = starts[1:] + [wide * LANES]
    lanes = [pl.ds(start, stop - start) for start, stop in zip(starts, stops)]
    assert len(lanes) <= piece
    early, late = range(2), range(2, len(lanes))

    def strip_at(spot):
        spot = lax.rem(spot + 2 * count, count)
        return pl.ds(pl.multiple_of(spot * strip, 16), strip)

    def held_at(first, step, k):
        rows = pl.ds(pl.multiple_of(first + step * strip, 16), strip)
        return gram.at[rows, pl.ds(width + lanes[k].start, lanes[k].size)]

    def ring_copy(step, k, source):
        return remote(
            source, held_at(block, step, k), ring_send.at[k, step], ring_recv.at[k, step],
            {"col": ring_column(place + ways[k % 2], count)},
        )

    def ring_start(streams):
        for k in streams:
            ring_copy(0, k, partial.at[strip_at(place - ways[k % 2]), lanes[k]]).start()

    def ring_step(step, streams):
        for k in streams:
            landed, running = held_at(block, step, k), held_at(running_rows, step, k)
            ring_copy(step, k, landed).wait_recv()
            mine = partial[strip_at(place - ways[k % 2] * (step + 2)), lanes[k]]
            value = landed[...].astype(jnp.float32) + mine.astype(jnp.float32)
            value = value.astype(jnp.bfloat16)

            @pl.when(step < count - 2)
            def _():
                running[...] = value
                ring_copy(step + 1, k, running).start()

            @pl.when(step == count - 2)
            def _():
                share[:, lanes[k]] = value

    @pl.loop(0, 4 * chunks)
    def _(event):
        slot, chunk = lax.div(event, chunks), lax.rem(event, chunks)
        for j in range(2):
            @pl.when(slot == 2 + j)
            def _():
                across(j, chunk).wait_recv()
                beside(j, chunk, core).start()

        @pl.when(event == 2 * chunks)
        def _():
            @pl.when(core == 0)
            def _():
                ring_start(early)

        @pl.when(event == 3 * chunks)
        def _():
            @pl.when(core == 0)
            def _():
                ring_start(late)

            @pl.when(core == 1)
            def _():
                ring_start(early)

        for j in range(2):
            @pl.when(slot == 2 + j)
            def _():
                beside(j, chunk, 1 - core).wait_recv()

        rows = pl.ds(pl.multiple_of(event * LANES, LANES), LANES)
        partner_row = 2 * chip + 1 - core
        far_row = 2 * (1 - chip) + slot - 2
        owner = jnp.where(slot == 0, me, jnp.where(slot == 1, partner_row, far_row))
        target = pl.ds(pl.multiple_of((owner * chunks + chunk) * LANES, LANES), LANES)
        mine = pl.ds(pl.multiple_of(me * slab_width, LANES), slab_width)
        slab[:, target] = gram[rows, mine].T
        skipped = jnp.where(core == 0, slot == 3, slot == 1)
        spot = chunk + chunks * jnp.where(core == 0, slot, lax.max(slot - 1, 0))

        @pl.when(jnp.logical_not(skipped))
        def _():
            value = outer_rows(gram[0:block, 0:width], gram[rows, 0:width])
            value = value.astype(jnp.bfloat16)
            for i in range(chunks):
                place_in = spot - i

                @pl.when((place_in >= 0) & (place_in < wide))
                def _():
                    into = pl.ds(pl.multiple_of(place_in * LANES, LANES), LANES)
                    held = slice(i * LANES, (i + 1) * LANES)
                    partial[held, into] = value[held]

        @pl.when(jnp.where(core == 0, slot == 2, slot == 3))
        def _():
            ring_step(chunk, early)

        @pl.when(jnp.where(core == 0, slot == 3, False))
        def _():
            ring_step(chunk, late)

    @pl.when(core == 1)
    def _():
        ring_start(late)

        @pl.loop(0, count - 1)
        def _(step):
            ring_step(step, late)

    def sent():
        for chunk in range(chunks):
            to_partner(chunk).wait_send()
            for j in range(2):
                across(j, chunk).wait_send()
                beside(j, chunk, core).wait_send()
        for step in range(count - 1):
            for k in range(len(lanes)):
                ring_copy(step, k, held_at(running_rows, step, k)).wait_send()

    return sent


def gather_plan(count):
    hops = (count // 2, count - 1 - count // 2)
    ring = [(w, s) for s in range(1, hops[0] + 1) for w in (0, 1) if s <= hops[w]]
    first = [("a",) + hop for hop in ring]
    second = [("b", x) + hop for hop in ring for x in (0, 1)]
    second.sort(key=lambda m: (m[3], m[1], m[2]))
    third = [("ya", 0, 0)] + [("ya",) + hop for hop in ring]
    order = [first[0], first[1], ("start_b",), ("yb",), third[0]]
    order += [first[2], first[3], third[1]]
    rest = first[4:]
    index = 2
    while second or rest:
        for source in (rest, second):
            order += source[:2]
            del source[:2]
        order += third[index : index + 1]
        index += 1
    return hops, order + third[index:]


def gather_names(count):
    _, order = gather_plan(count)
    arrivals = [m for m in order if m[0] != "start_b"]
    partner = [("p",) + m for m in arrivals] + [("p", "own_a"), ("p", "own_b")]
    return {name: number for number, name in enumerate(arrivals + partner)}


def strip_names(bits, u):
    if u == 0:
        near = [[], [("ya", 0, 0), ("yb",)]][bits // 2]
        if bits == 1:
            return [("p", "own_a"), ("p", "own_b")]
    else:
        w, s = (0, -u) if u < 0 else (1, u)
        near = [("ya" if bits & 2 else "a", w, s), ("b", bits // 2, w, s)]
    return [("p",) + m for m in near] if bits & 1 else near


def gather_groups(count, width):
    (long, short), order = gather_plan(count)
    works = []
    for bits in range(4):
        for u in range(-long, short + 1):
            after = u + 1 if u < short else -long
            works.append((bits, u, strip_names(bits, u) + strip_names(bits, after)))
    seen = set()
    groups = []
    for start in range(0, len(order), width):
        events = order[start : start + width]
        due = set(seen)
        seen.update(events)
        ready = []
        for work in list(works):
            names = [m[1:] if m[0] == "p" else m for m in work[2]]
            known = due if work[0] & 1 else seen
            if all(m in known or m[0] in ("own_a", "own_b") for m in names):
                works.remove(work)
                ready.append(work)
        groups.append((events, ready))
    groups.append(([], works))
    return groups


def gather_steps(count, head, strip, land, send_sems, recv_sems):
    me, column = lax.axis_index("row"), lax.axis_index("col")
    place = ring_place(column, count)
    sign = 1 - 2 * lax.rem(me, 2)
    ways = (sign, -sign)
    hops, _ = gather_plan(count)
    names = gather_names(count)

    def where(name, mirrored=False):
        kind = name[0]
        if kind == "p":
            return where(name[1:], True)
        w, s, bits, part = 0, 0, 0, kind[-1]
        if kind in ("a", "ya"):
            w, s = name[1], name[2]
            bits = 2 if kind == "ya" else 0
        elif kind == "b":
            bits, w, s = 2 * name[1], name[2], name[3]
        elif kind == "yb":
            bits = 2
        if mirrored:
            bits = bits + 1
        way = -ways[w] if mirrored else ways[w]
        spot = lax.rem(place - way * s + count, count)
        start = (flipped(me, bits) * count + spot) * strip
        if part == "b":
            return land.at[pl.ds(pl.multiple_of(start + head, 16), strip - head)]
        return land.at[pl.ds(pl.multiple_of(start, 16), head)]

    def target(name):
        if name[0] == "p":
            return {"row": flipped(me, 1)}
        if name[0] in ("ya", "yb"):
            return {"row": flipped(me, 2)}
        w = name[1] if name[0] == "a" else name[2]
        return {"col": ring_column(place + ways[w], count)}

    def copy_of(name, source):
        number = names[name]
        return remote(source, source, send_sems.at[number], recv_sems.at[number], target(name))

    def send(name, held):
        copy_of(name, held).start()

    own_a, own_b = where(("own_a",)), where(("own_b",))

    def begin():
        send(("a", 0, 1), own_a)
        send(("a", 1, 1), own_a)
        send(("yb",), own_b)
        send(("ya", 0, 0), own_a)
        send(("p", "own_a"), own_a)
        send(("p", "own_b"), own_b)

    def arrive(name):
        if name[0] == "start_b":
            send(("b", 0, 0, 1), own_b)
            send(("b", 0, 1, 1), own_b)
            return
        held = where(name)
        copy_of(name, held).wait_recv()
        if name[0] == "a":
            w, s = name[1:]
            if s < hops[w]:
                send(("a", w, s + 1), held)
            send(("ya", w, s), held)
        elif name[0] == "b":
            x, w, s = name[1:]
            if s < hops[w]:
                send(("b", x, w, s + 1), held)
        elif name[0] == "yb":
            send(("b", 1, 0, 1), held)
            send(("b", 1, 1, 1), held)
        send(("p",) + name, held)

    def land_from_partner(name):
        copy_of(name, where(name)).wait_recv()

    def sent():
        for name in names:
            kind = name[1] if name[0] == "p" else name[0]
            copy_of(name, own_a if kind[-1] == "a" else own_b).wait_send()

    return begin, arrive, land_from_partner, sent


def update_kernel(
    count, factor, head, base_ref, out_ref, gram, land, slab_ref, first, rough, exact,
    stage, total, partial, sends, recvs, own_sem, free_sem, out_send, out_recv,
    panel_send, panel_recv, ring_send, ring_recv,
):
    size = gram.shape[0]
    blocks = size // LANES
    strip = size // 4 // count
    wide = land.shape[1] // LANES
    width = slab_ref.shape[0]
    tile = 512 if size % 512 == 0 else LANES
    block = size // 4
    chunks = block // LANES
    me, column = lax.axis_index("row"), lax.axis_index("col")
    place = ring_place(column, count)
    sign = 1 - 2 * lax.rem(me, 2)
    number = me * count + place
    ring = [{"col": ring_column(place + way, count)} for way in (1, -1)]
    near = ring + [{"row": flipped(me, bits)} for bits in (1, 2)]
    meet(pltpu.get_barrier_semaphore(), near + [{"row": flipped(me, 3)}])

    def column_block(index):
        return pl.ds(pl.multiple_of(lax.rem(index, blocks) * LANES, LANES), LANES)

    mine_rows = pl.ds(pl.multiple_of(number * strip, 16), strip)

    def place_block(i, squares):
        here = column_block(i)
        single = double = jnp.zeros((8, LANES), jnp.float32)
        for d in range(wide):
            piece = land[here, d * LANES : (d + 1) * LANES]
            there = column_block(i + d)
            gram[here, there] = piece
            if 0 < d < wide - 1:
                gram[there, here] = piece.T
            if squares:
                value = piece.astype(jnp.float32)
                value = jnp.sum((value * value).reshape(LANES // 8, 8, LANES), axis=0)
                if 0 < d < wide - 1:
                    double = double + value
                else:
                    single = single + value
        if squares:
            total[...] += single + 2.0 * double

    def place_blocks(works, squares):
        if not works:
            return

        @pl.loop(0, len(works))
        def _(step):
            bits, u = works[0][:2]
            code = jnp.int32(bits * 2 * count + u + count)
            for k, (bits, u, _) in enumerate(works[1:], 1):
                code = jnp.where(step == k, bits * 2 * count + u + count, code)
            bits, u = lax.div(code, 2 * count), lax.rem(code, 2 * count) - count
            high, low = lax.div(bits, 2), lax.rem(bits, 2)
            chip, core = lax.div(me, 2), lax.rem(me, 2)
            row = 2 * (chip + high - 2 * chip * high) + (core + low - 2 * core * low)
            way = sign * (1 - 2 * low)
            spot = lax.rem(place + way * u + lax.div(way - 1, 2) + 2 * count, count)

            @pl.when(spot < chunks)
            def _():
                place_block(row * chunks + spot, squares)

    summed_out = sum_share(
        count, wide, base_ref, slab_ref, gram, partial, land.at[mine_rows],
        block + strip * count, panel_send, panel_recv, own_sem, ring_send, ring_recv,
    )
    total[...] = jnp.zeros_like(total)

    def run_groups(groups, steps, squares):
        _, arrive, land_from_partner, sent = steps
        waited = set()
        for events, works in groups:
            for name in events:
                arrive(name)
            for _, _, names in works:
                for name in names:
                    if name[0] == "p" and name not in waited:
                        waited.add(name)
                        land_from_partner(name)
            place_blocks(works, squares)
        sent()

    steps = gather_steps(count, head, strip, land, sends.at[0], recvs.at[0])
    steps[0]()
    summed_out()
    run_groups(gather_groups(count, 3), steps, True)
    for target in near:
        pl.semaphore_signal(
            free_sem, inc=1, device_id=target, device_id_type=pl.DeviceIdType.MESH
        )
    quartic = jnp.sum(jnp.sum(total[...], axis=0, keepdims=True), axis=1, keepdims=True)
    scale = 1.0 / jnp.sqrt(jnp.sqrt(quartic) + EPSILON)
    square = scale * scale

    def times_gram(source, finish, hooks=(), begin=0, tiles=size // tile):
        @pl.loop(0, tiles)
        def _(step):
            for k, calls in enumerate(hooks):
                if calls:
                    @pl.when(step == k)
                    def _():
                        for call in calls:
                            call()

            at = lax.rem(begin + step, size // tile)
            columns = pl.ds(pl.multiple_of(at * tile, tile), tile)
            finish(
                columns,
                jnp.dot(source[...], gram[:, columns], preferred_element_type=jnp.float32),
            )

    part = exact.at[pl.ds(0, strip)]
    left, right = rough.at[pl.ds(0, strip)], first.at[pl.ds(0, strip)]
    mine = gram.at[mine_rows]

    def after_square(columns, value):
        value = value * square * square
        part[:, columns] = (
            COEF_LINEAR * (mine[:, columns].astype(jnp.float32) * square)
            + COEF_CUBIC * value
        )
        left[:, columns] = value.astype(jnp.bfloat16)

    def after_cube(columns, value):
        right[:, columns] = (
            part[:, columns] + COEF_QUINTIC * (value * square)
        ).astype(jnp.bfloat16)

    def after_third(columns, value):
        value = value * square
        part[:, columns] = (
            COEF_LINEAR * right[:, columns].astype(jnp.float32) + COEF_CUBIC * value
        )
        left[:, columns] = value.astype(jnp.bfloat16)

    times_gram(mine, after_square)
    times_gram(left, after_cube)
    times_gram(right, after_third)
    times_gram(
        left,
        after_cube,
        begin=lax.div(number * strip, tile),
        tiles=min(size // tile, pl.cdiv((wide + 1) * LANES, tile) + 1),
    )

    pl.semaphore_wait(free_sem, len(near))
    for group in range(strip // 16):
        sixteenth = number * (strip // 16) + group
        base = lax.div(sixteenth, LANES // 16)
        rows = pl.ds(pl.multiple_of(sixteenth * 16, 16), 16)
        for t in range(wide):
            land[rows, t * LANES : (t + 1) * LANES] = right[
                group * 16 : group * 16 + 16, column_block(base + t)
            ]

    steps = gather_steps(count, head, strip, land, sends.at[1], recvs.at[1])
    steps[0]()
    groups = gather_groups(count, 3)
    slots = size // tile
    paced = [[] for _ in range(2 * slots)]
    early, waiting = [], []
    for k, (events, works) in enumerate(groups):
        if len(early) + len(events) <= 21:
            early += events
            waiting += works
            groups[k] = ([], [])
        else:
            groups[k] = (events, waiting + works)
            break
    for k, name in enumerate(early):
        paced[slots // 2 + k * (2 * slots - slots // 2) // len(early)].append(
            functools.partial(steps[1], name)
        )

    def keep(columns, value):
        value = value * square
        exact[:, columns] = (
            COEF_LINEAR * slab_ref[:, columns].astype(jnp.float32) + COEF_CUBIC * value
        )
        rough[:, columns] = value.astype(jnp.bfloat16)

    def combine(columns, value):
        first[:, columns] = (
            exact[:, columns] + COEF_QUINTIC * (value * square)
        ).astype(jnp.bfloat16)

    times_gram(slab_ref, keep, paced[:slots])
    times_gram(rough, combine, paced[slots:])
    run_groups(groups, steps, False)

    def out_copy(bits, part):
        lanes = pl.ds(pl.multiple_of(me * width + part * LANES, LANES), LANES)
        held = pl.ds(pl.multiple_of(part * LANES, LANES), LANES)
        return remote(
            stage.at[bits, :, held],
            out_ref.at[:, lanes],
            out_send.at[bits - 1, part],
            out_recv.at[bits - 1, part],
            {"row": flipped(me, bits)},
        )

    @pl.loop(0, width // LANES)
    def _(index):
        part = pl.ds(pl.multiple_of(index * LANES, LANES), LANES)

        def after_product(columns, value):
            exact[part, columns] = (
                COEF_LINEAR * first[part, columns].astype(jnp.float32) + COEF_CUBIC * value
            )
            rough[part, columns] = value.astype(jnp.bfloat16)

        times_gram(first.at[part], after_product)

        @pl.loop(0, 4)
        def _(step):
            bits = 3 - step
            chip, core = lax.div(me, 2), lax.rem(me, 2)
            high, low = lax.div(bits, 2), lax.rem(bits, 2)
            owner = 2 * (chip + high - 2 * chip * high) + (core + low - 2 * core * low)
            columns = pl.ds(pl.multiple_of(owner * block, LANES), block)
            value = jnp.dot(
                rough[part, :], gram[:, columns], preferred_element_type=jnp.float32
            )
            value = (exact[part, columns] + COEF_QUINTIC * value) * (scale * factor)
            stage[bits, :, part] = value.astype(jnp.bfloat16).T
            for x in range(1, 4):
                @pl.when(bits == x)
                def _():
                    out_copy(x, index).start()

    lanes = pl.ds(pl.multiple_of(me * width, LANES), width)
    kept = pltpu.make_async_copy(stage.at[0], out_ref.at[:, lanes], own_sem)
    kept.start()
    kept.wait()
    for bits in range(1, 4):
        for part in range(width // LANES):
            out_copy(bits, part).wait()


def updated(base, factor, count, wide):
    block, full_width = base.shape
    size, width = 4 * block, full_width // 4
    strip = block // count
    head = strip * 4 // 7 // 16 * 16
    chunks = block // LANES
    half = pltpu.VMEM((width, size), jnp.bfloat16)
    messages = len(gather_names(count))
    dma = pltpu.SemaphoreType.DMA
    return pl.pallas_call(
        functools.partial(update_kernel, count, factor, head),
        out_shape=jax.ShapeDtypeStruct((block, full_width), jnp.bfloat16),
        in_specs=[pl.BlockSpec(memory_space=pl.ANY)],
        out_specs=pl.BlockSpec(memory_space=pl.ANY),
        scratch_shapes=[
            pltpu.VMEM((size, size), jnp.bfloat16),
            pltpu.VMEM((size, wide * LANES), jnp.bfloat16),
            half,
            half,
            half,
            pltpu.VMEM((width, size), jnp.float32),
            pltpu.VMEM((4, block, width), jnp.bfloat16),
            pltpu.VMEM((8, LANES), jnp.float32),
            pltpu.VMEM((block, wide * LANES), jnp.bfloat16),
            dma((2, messages)),
            dma((2, messages)),
            dma,
            pltpu.SemaphoreType.REGULAR,
            dma((3, width // LANES)),
            dma((3, width // LANES)),
            dma((5, chunks)),
            dma((5, chunks)),
            dma((6, count - 1)),
            dma((6, count - 1)),
        ],
        compiler_params=pltpu.CompilerParams(
            collective_id=1, has_side_effects=True, vmem_limit_bytes=63 * 1024 * 1024
        ),
        name="updated",
    )(base)


def per_device(factor, gradient, momentum):
    rows = lax.axis_size("row")
    grad32 = gradient.astype(jnp.float32)
    buffer = MOMENTUM_DECAY * momentum + grad32
    nesterov = grad32 + MOMENTUM_DECAY * buffer
    base = nesterov.astype(jnp.bfloat16)
    block = base.shape[0]
    count = lax.axis_size("col")
    strip = block // count
    if (
        rows == 4
        and count % 2 == 0
        and count >= 4
        and block % LANES == 0
        and base.shape[1] % (4 * LANES) == 0
        and strip * count == block
        and strip % 16 == 0
        and 32 <= strip < LANES
        and block // LANES + 1 == count
        and base.shape[1] + (2 * block // LANES + 1) * LANES <= 4 * block
    ):
        wide = 4 * block // LANES // 2 + 1
        return (updated(base, factor, count, wide), buffer)
    half = block // 2
    middle = rows // 2
    me = lax.axis_index("row")
    panel = lax.all_gather(base, "row", axis=0, tiled=True)

    def rows_of(offset):
        start = ((me + offset) % rows) * block
        return lax.dynamic_slice_in_dim(panel, start, block, axis=0)

    parts = [outer_rows(base, base)]
    for offset in range(1, middle):
        parts.append(outer_rows(rows_of(offset), base))
    facing = rows_of(middle)
    lower = me < middle
    parts.append(
        outer_rows(
            jnp.where(lower, base[:half], facing[half:]), jnp.where(lower, facing, base)
        )
    )
    partial_value = jnp.concatenate([part.astype(jnp.bfloat16) for part in parts], axis=0)
    count = lax.axis_size("col")
    if block % 128 or count % 2 or count < 4:
        share = lax.psum_scatter(partial_value, "col", scatter_dimension=0, tiled=True)
    else:
        share = ring_sum(partial_value, count)
    shares = lax.all_gather(share, ("row", "col"), axis=0, tiled=True)
    parts = rows
    if block % 128:
        shares = assembled(shares.reshape(rows, -1, block), rows, block)
        parts = 1

    width = panel.shape[1] // rows
    slab = lax.dynamic_slice_in_dim(panel, me * width, width, axis=1)
    update = chain(shares, slab, factor, parts)
    update = lax.all_to_all(update, "row", 0, 1, tiled=True)
    return (update, buffer)


def solution(mesh):
    def whole(gradient, momentum):
        factor = 0.2 * math.sqrt(max(gradient.shape))
        return jax.shard_map(
            functools.partial(per_device, factor),
            mesh=mesh,
            in_specs=(P("row", "col"), P("row", "col")),
            out_specs=(P("row", "col"), P("row", "col")),
            check_vma=False,
        )(gradient, momentum)

    return whole
```
